32 devices in a mesh: depth: 2 (over y), lat: 8 (over z, x), freq: 2 (over core).
Axes of the slice: x: 2, y: 2, z: 4, core: 2. Of those that a mesh axis runs over, the one named last changes fastest.
Arguments:
- surface: bfloat16 [6, 2, 128, 8192], P('freq', None, None, 'lat'), may hold values from -6 to 6
- refl: float32 [2, 8192], P('depth', 'lat'), may hold values from -0.5 to 0.5
- pool: bfloat16 [2, 6, 8, 128, 256], P('depth', 'freq'), may hold values from -0.375 to 0.375
- tile_ids: int32 [2, 64, 10], P('depth', 'lat'), may hold values from 0 to 63, as said below
- block_ids: int32 [2, 64, 10], P('depth', 'lat'), may hold values from 0 to 7
- counts: int32 [2, 64], P('depth', 'lat'), may hold values from 1 to 10, as said below
Outputs:
- image: float32 [2, 8192], P('depth', 'lat')
The draws below stay inside these ranges and needn't reach their ends.
Inputs may be any that keep to these rules, and one draw needn't show every extreme that they name: tile_ids[l, j, k] = (j + o) mod 64 for an offset o with -8 <= o <= 8; slot 0 names the row's own tile; in every level some row has all 10 slots live with offsets 8 at slot 1 and -8 at slot 2. Slots k >= counts[l, j] of row j are padding; in every level some row has all 10 slots live.
All inputs are finite; a program needn't handle non-finite values.
Results may differ from the reference program's by a relative error of at most 0.00055.
Values may be sent and summed in bfloat16 or wider, within the bound.
No kernel may reach another device: no remote copies, remote signals or barrier semaphores. Data moves between devices by JAX's collectives and lax.ppermute only.
A program may use at most 128 MiB of HBM per device.

```python
import jax
import jax.numpy as jnp
from jax import lax

TILE = 128
SLOTS = 10
POOL = 8
TILE_DEV = 8
SHOTS = 128
LEVELS = 2
FREQS = 6
TILES = 64
NX = 8192
APER = 8


def aperture_lists(key):
    offset_key = jax.random.fold_in(key, 11)
    row_key = jax.random.fold_in(key, 12)
    heavy_key = jax.random.fold_in(key, 13)
    base_key = jax.random.fold_in(key, 14)
    extra_key = jax.random.fold_in(key, 15)
    offsets = jax.random.randint(offset_key, (LEVELS, TILES, SLOTS), -APER, APER + 1)
    slot_index = jnp.arange(SLOTS)[None, None, :]
    row_index = jnp.arange(TILES)[None, :, None]
    chosen_row = jax.random.randint(row_key, (LEVELS,), 0, TILES)
    is_chosen = jnp.arange(TILES)[None, :] == chosen_row[:, None]
    offsets = jnp.where(slot_index == 0, 0, offsets)
    offsets = jnp.where(is_chosen[:, :, None] & (slot_index == 1), APER, offsets)
    offsets = jnp.where(is_chosen[:, :, None] & (slot_index == 2), -APER, offsets)
    tile_lists = jnp.mod(row_index + offsets, TILES).astype(jnp.int32)
    heavy_region = (jax.random.randint(heavy_key, (LEVELS, TILES // TILE_DEV), 0, 4) == 0).astype(jnp.int32)
    heavy_rows = jnp.repeat(heavy_region, TILE_DEV, axis=1)
    base_count = 3 + jax.random.randint(base_key, (LEVELS, TILES), 0, 3)
    extra_count = jax.random.randint(extra_key, (LEVELS, TILES), 0, SLOTS - 4)
    live_counts = jnp.where(is_chosen, SLOTS, base_count + heavy_rows * extra_count).astype(jnp.int32)
    return (tile_lists, live_counts)


def draw_tile_ids(key, part):
    return aperture_lists(key)[0]


def draw_counts(key, part):
    return aperture_lists(key)[1]


def plant(array, key, least, high):
    spot = [jax.random.randint(jax.random.fold_in(key, axis), (), 0, length) for axis, length in enumerate(array.shape)]
    main_axis = array.shape.index(max(array.shape))
    neighbour = spot[:main_axis] + [(spot[main_axis] + 1) % array.shape[main_axis]] + spot[main_axis + 1:]
    return array.at[tuple(spot)].set(least).at[tuple(neighbour)].set(high)


def shard_levels(key, dims, shards, smallest, largest):
    factor_of = 1.0
    for position, parts in shards:
        draws = jax.random.uniform(jax.random.fold_in(jax.random.fold_in(key, 6), position), (parts,), jnp.float32, smallest / len(shards), largest / len(shards))
        factor_of = factor_of * jnp.repeat(jnp.exp(draws), dims[position] // parts).reshape((-1,) + (1,) * (len(dims) - 1 - position))
    return factor_of


def normal_values(own_key, extent, deviation, reach, cuts=(), kind=jnp.bfloat16):
    level = shard_levels(own_key, extent, cuts, -0.22, 0.18) if cuts else 1.0
    drawn = jax.random.normal(own_key, extent, jnp.float32) * deviation * level
    return jnp.minimum(jnp.maximum(drawn, -reach), reach).astype(kind)


def setup_inputs(seed: int = 0) -> dict:
    streams_of = jax.random.split(jax.random.key(seed), 7)
    surface = normal_values(streams_of[0], (FREQS, 2, SHOTS, NX), 1.0, 6.0, ((0, 2), (3, 8)))
    refl = jnp.clip(jax.random.uniform(streams_of[1], (LEVELS, NX), jnp.float32, -0.5, 0.5) * shard_levels(streams_of[1], (LEVELS, NX), ((0, 2), (1, 8)), -0.4, 0.0), -0.5, 0.5)
    pool = normal_values(streams_of[2], (LEVELS, FREQS, POOL, TILE, 2 * TILE), (2 * TILE) ** -0.5, 0.375, ((0, 2), (1, 2)))
    tile_ids = draw_tile_ids(jax.random.fold_in(streams_of[6], 71), 0)
    block_ids = plant(jax.random.randint(streams_of[4], (LEVELS, TILES, SLOTS), 0, POOL), jax.random.fold_in(streams_of[4], 1), 0, POOL - 1).astype(jnp.int32)
    counts = draw_counts(jax.random.fold_in(streams_of[6], 71), 0)
    return dict(surface=surface, refl=refl, pool=pool, tile_ids=tile_ids, block_ids=block_ids, counts=counts)


def advance(wave_field, pool_level, ids_level, blocks_level, counts_level, refl_level):
    tile_grid = wave_field.reshape(FREQS, 2, SHOTS, TILES, TILE)
    slot_index = jnp.arange(SLOTS, dtype=jnp.int32)

    def one_row(row_args):
        row_ids, row_blocks, row_count = row_args
        slot_live = (slot_index < row_count).astype(jnp.float32)
        picked = jnp.take(tile_grid, row_ids.astype(jnp.int32), axis=3).astype(jnp.float32)
        picked = picked * slot_live[None, None, None, :, None]
        chosen = jnp.take(pool_level, row_blocks.astype(jnp.int32), axis=1).astype(jnp.float32)
        product = jnp.einsum('fsakt,fktc->fsac', picked, chosen)
        real_part = product[:, 0, :, :TILE] - product[:, 1, :, TILE:]
        imag_part = product[:, 0, :, TILE:] + product[:, 1, :, :TILE]
        row_scale = 1.0 / jnp.sqrt(row_count.astype(jnp.float32))
        return jnp.stack([real_part, imag_part], 1) * row_scale
    rows_out = lax.map(one_row, (ids_level, blocks_level, counts_level))
    wave_out = jnp.transpose(rows_out, (1, 2, 3, 0, 4)).reshape(FREQS, 2, SHOTS, NX)
    wave_out = wave_out * (1.0 - refl_level)
    level_image = lax.optimization_barrier(jnp.sum(wave_out * wave_out, axis=(0, 1, 2))) / (FREQS * SHOTS)
    return (wave_out.astype(jnp.bfloat16), level_image)

def reference(surface, refl, pool, tile_ids, block_ids, counts):
    wave_field = surface
    images = []
    for level_index in range(LEVELS):
        wave_field, level_image = advance(wave_field, pool[level_index], tile_ids[level_index], block_ids[level_index], counts[level_index], refl[level_index])
        images.append(level_image)
    return jnp.stack(images, 0)
```

```python
import functools

import jax
import jax.numpy as jnp
from jax import lax
from jax.experimental import pallas as pl
from jax.experimental.pallas import tpu as pltpu
from jax.sharding import PartitionSpec as P

TILE = 128
TILE_DEV = 8


def extended_2(block, sides, width):
    for axis, dim in sides:
        count = lax.axis_size(axis)
        forward = [(i, i + 1) for i in range(count - 1)]
        forward.append((count - 1, 0))
        backward = [(target, source) for source, target in forward]
        low = lax.ppermute(
            lax.slice_in_dim(block, block.shape[dim] - width, None, axis=dim), axis, forward
        )
        high = lax.ppermute(lax.slice_in_dim(block, 0, width, axis=dim), axis, backward)
        block = jnp.concatenate([low, block, high], axis=dim)
    return block


def aperture_rim(wave_field):
    return extended_2(wave_field, (("lat", 3),), TILE_DEV * TILE)


def extrapolate(extended, pool_level, local_ids, block_level, count_level, refl_level):
    freqs_here = extended.shape[0]
    shot_rows = extended.shape[2]
    tile_rows = local_ids.shape[0]
    slot_total = local_ids.shape[1]
    tile_grid = extended.reshape(freqs_here, 2, shot_rows, -1, TILE)
    slot_live = (jnp.arange(slot_total)[None, :] < count_level[:, None]).astype(jnp.bfloat16)
    picked = jnp.take(tile_grid, local_ids, axis=3) * slot_live[None, None, None, :, :, None]
    chosen = jnp.take(pool_level, block_level, axis=1)
    product = jnp.einsum("fsarkt,frktc->rfsac", picked, chosen, preferred_element_type=jnp.float32)
    real_part = product[:, :, 0, :, :TILE] - product[:, :, 1, :, TILE:]
    imag_part = product[:, :, 0, :, TILE:] + product[:, :, 1, :, :TILE]
    row_scale = 1.0 / jnp.sqrt(count_level.astype(jnp.float32))
    rows_out = jnp.stack([real_part, imag_part], 2) * row_scale[:, None, None, None, None]
    wave_out = jnp.transpose(rows_out, (1, 2, 3, 0, 4)).reshape(
        freqs_here, 2, shot_rows, tile_rows * TILE
    )
    wave_out = wave_out * (1.0 - refl_level)
    return (wave_out.astype(jnp.bfloat16), jnp.sum(wave_out * wave_out, axis=(0, 1, 2)))


def per_device(surface, refl, pool, tile_ids, block_ids, counts):
    depth_index = lax.axis_index("depth")
    lat_index = lax.axis_index("lat")
    tile_count = TILE_DEV * lax.axis_size("lat")
    first_tile = lat_index * TILE_DEV - TILE_DEV
    freqs_here = surface.shape[0]
    shot_total = surface.shape[2]
    lateral_width = surface.shape[3]
    shot_rows = shot_total // lax.axis_size("depth")
    own_shots = lax.dynamic_slice_in_dim(surface, depth_index * shot_rows, shot_rows, 2)
    pool_all = lax.all_gather(pool, "depth", axis=0, tiled=True)
    ids_all, blocks_all, counts_all = (
        lax.all_gather(tile_ids, "depth", axis=0, tiled=True),
        lax.all_gather(block_ids, "depth", axis=0, tiled=True),
        lax.all_gather(counts, "depth", axis=0, tiled=True),
    )
    refl_all = lax.all_gather(refl, "depth", axis=0, tiled=True)
    level_total = pool_all.shape[0]

    def level_step(level_index, loop_state):
        wave_field, images = loop_state
        ids_here = lax.dynamic_index_in_dim(ids_all, level_index, 0, keepdims=False)
        local_level = jnp.mod(ids_here - first_tile, tile_count)
        pool_here = lax.dynamic_index_in_dim(pool_all, level_index, 0, keepdims=False)
        blocks_here = lax.dynamic_index_in_dim(blocks_all, level_index, 0, keepdims=False)
        counts_here = lax.dynamic_index_in_dim(counts_all, level_index, 0, keepdims=False)
        refl_here = lax.dynamic_index_in_dim(refl_all, level_index, 0, keepdims=False)
        handed, partial_value = extrapolate(
            aperture_rim(wave_field), pool_here, local_level, blocks_here, counts_here, refl_here
        )
        images = lax.dynamic_update_index_in_dim(images, partial_value, level_index, 0)
        return (handed, images)

    start_images = jnp.zeros((level_total, lateral_width), jnp.float32)
    loop_state = lax.fori_loop(0, level_total, level_step, (own_shots, start_images))
    image_local = lax.psum_scatter(loop_state[1], "depth", scatter_dimension=0, tiled=True)[0]
    summed = lax.psum(image_local, "freq")
    divisor = freqs_here * lax.axis_size("freq") * shot_total
    return (summed / divisor)[None, :]


HALF = TILE // 2
VMEM_SPACE = pl.BlockSpec(memory_space=pltpu.VMEM)
ANY_SPACE = pl.BlockSpec(memory_space=pl.ANY)


def pack_kernel(lat_size, depth_ref, surface_ref, tables_ref, out_ref, own_buf, half_buf, sems):
    depth_index = depth_ref[0]
    half_shots = half_buf.shape[1]
    shots_own = own_buf.shape[1] // lat_size
    shots_half = half_shots // lat_size
    tiles = own_buf.shape[2] // TILE
    own_copy = pltpu.make_async_copy(surface_ref.at[2 * depth_index], own_buf, sems.at[0])
    half_copy = pltpu.make_async_copy(
        surface_ref.at[1, :, pl.ds(depth_index * half_shots, half_shots), :], half_buf, sems.at[1]
    )
    own_copy.start()
    half_copy.start()
    base_half = tiles * shots_own
    base_table = base_half + tiles * shots_half
    refl = tables_ref[0, :tiles, :]
    high = refl.astype(jnp.bfloat16).astype(jnp.float32)
    rest = refl - high
    middle = rest.astype(jnp.bfloat16).astype(jnp.float32)
    low = rest - middle
    lists = tables_ref[0, tiles:, :] + pltpu.roll(tables_ref[1, tiles:, :], HALF, 1)
    rows_left = jnp.concatenate([high, low], axis=0).astype(jnp.bfloat16)
    rows_right = jnp.concatenate([middle, lists], axis=0).astype(jnp.bfloat16)
    for target in range(lat_size):
        out_ref[target, base_table:, :TILE] = rows_left
        out_ref[target, base_table:, TILE:] = rows_right
    own_copy.wait()
    for target in range(lat_size):
        for part in range(2):
            for tile in range(tiles):
                out_ref[
                    target, tile * shots_own:(tile + 1) * shots_own, part * TILE:(part + 1) * TILE
                ] = own_buf[
                    part, target * shots_own:(target + 1) * shots_own, tile * TILE:(tile + 1) * TILE
                ]
    half_copy.wait()
    for pair in range(lat_size // 2):
        for part in range(2):
            for tile in range(0, tiles, 2):
                rows = slice(pair * 2 * shots_half, (pair + 1) * 2 * shots_half)
                even = half_buf[part, rows, tile * TILE:(tile + 1) * TILE].astype(jnp.float32)
                odd = half_buf[part, rows, (tile + 1) * TILE:(tile + 2) * TILE].astype(jnp.float32)
                start = base_half + tile * shots_half
                lanes = slice(part * TILE, (part + 1) * TILE)
                for side in range(2):
                    part_rows = slice(side * shots_half, (side + 1) * shots_half)
                    joined = jnp.concatenate([even[part_rows], odd[part_rows]], axis=0)
                    out_ref[2 * pair + side, start:start + 2 * shots_half, lanes] = joined.astype(
                        jnp.bfloat16
                    )


def level_kernel(
    shots, row_start, levels, slots, index_ref, scale_ref, wave_ref, local_ref, remote_ref,
    image_in_ref, depth_ref, freq_ref, image_ref, pool_buf, table, wave_buf, pass_buf, sems,
):
    lat_size = wave_ref.shape[0]
    blocks = pool_buf.shape[1]
    tiles = table.shape[0] - 1
    entries = tiles // blocks
    per_source = entries // lat_size
    depth_index = depth_ref[0]
    freq_index = freq_ref[0]
    copies = [
        pltpu.make_async_copy(local_ref.at[0, freq_index], pool_buf.at[depth_index], sems.at[0]),
        pltpu.make_async_copy(remote_ref, pool_buf.at[1 - depth_index], sems.at[1]),
    ]
    for copy in copies:
        copy.start()
    rows_source = per_source * shots
    row_table = per_source * 24
    for source in range(lat_size):
        refl = (
            wave_ref[source, row_table:row_table + per_source, :TILE].astype(jnp.float32)
            + wave_ref[source, row_table:row_table + per_source, TILE:].astype(jnp.float32)
        ) + wave_ref[source, row_table + per_source:row_table + 2 * per_source, :TILE].astype(
            jnp.float32
        )
        pass_buf[source * per_source:(source + 1) * per_source, :] = 1.0 - refl
    table[tiles] = jnp.zeros(table.shape[1:], table.dtype)
    for copy in copies:
        copy.wait()
    sources_step = lat_size // 2

    for level in range(levels):
        last = level == levels - 1

        def block_step(block, carry):
            upper = pool_buf[level, block]
            lower = jnp.concatenate([-upper[:, TILE:], upper[:, :TILE]], axis=1)
            weights = jnp.concatenate([upper, lower], axis=0)
            for step in range(2):
                if level == 0:
                    left = wave_ref[
                        step * sources_step:(step + 1) * sources_step,
                        row_start:row_start + rows_source, :
                    ].reshape(sources_step * rows_source, 2 * TILE)
                else:
                    left = wave_buf[
                        step * sources_step * rows_source:(step + 1) * sources_step * rows_source, :
                    ]
                product = jnp.dot(left, weights, preferred_element_type=jnp.float32)
                count = sources_step * per_source
                table[pl.ds(block * entries + step * count, count)] = product.reshape(
                    count, shots, 2 * TILE
                )
            return carry

        lax.fori_loop(0, blocks, block_step, 0)
        rows_step = max(1, 16 // shots)

        def row_step(step, carry):
            outs = []
            for inner in range(rows_step):
                row = step * rows_step + inner
                base = (level * entries + row) * slots
                total = table[index_ref[base]]
                for slot in range(1, slots):
                    total = total + table[index_ref[base + slot]]
                total = total * scale_ref[level * entries + row]
                if not last:
                    kept = pass_buf[pl.ds(row, 1), :]
                    total = total * jnp.concatenate([kept, kept], axis=1)
                    outs.append(total)
                squares = total * total
                squares = squares[:, :TILE] + squares[:, TILE:]
                line = jnp.sum(squares, axis=0, keepdims=True)
                image_ref[pl.ds(level * entries + row, 1), :] = (
                    image_in_ref[pl.ds(level * entries + row, 1), :] + line
                )
            if not last:
                joined = jnp.concatenate(outs, axis=0) if rows_step > 1 else outs[0]
                height = rows_step * shots
                start = pl.multiple_of(step * height, height)
                wave_buf[pl.ds(start, height), :] = joined.astype(jnp.bfloat16)
            return carry

        lax.fori_loop(0, entries // rows_step, row_step, 0)


def run_levels(shots, row_start, index, scale, wave, local, remote, image, depth_id, freq_id):
    blocks = local.shape[2]
    levels = scale.shape[0]
    entries = scale.shape[1]
    slots = index.size // scale.size
    smem = pl.BlockSpec(memory_space=pltpu.SMEM)
    return pl.pallas_call(
        functools.partial(level_kernel, shots, row_start, levels, slots),
        out_shape=jax.ShapeDtypeStruct((levels * entries, TILE), jnp.float32),
        in_specs=[smem, smem, VMEM_SPACE, ANY_SPACE, ANY_SPACE, VMEM_SPACE, smem, smem],
        out_specs=VMEM_SPACE,
        scratch_shapes=[
            pltpu.VMEM((levels, blocks, TILE, 2 * TILE), jnp.bfloat16),
            pltpu.VMEM((blocks * entries + 1, shots, 2 * TILE), jnp.float32),
            pltpu.VMEM((entries * shots, 2 * TILE), jnp.bfloat16),
            pltpu.VMEM((entries, TILE), jnp.float32),
            pltpu.SemaphoreType.DMA((2,)),
        ],
        cost_estimate=pl.CostEstimate(
            flops=2 * levels * blocks * entries * shots * 4 * TILE * TILE,
            bytes_accessed=8 * entries * shots * TILE + 8 * blocks * TILE * TILE,
            transcendentals=0,
        ),
        name="levels_" + str(shots),
    )(index.reshape(-1), scale.reshape(-1), wave, local, remote, image, depth_id, freq_id)


def per_device_fast(surface, refl, pool, tile_ids, block_ids, counts):
    depth_index = lax.axis_index("depth")
    depth_size = lax.axis_size("depth")
    lat_size = lax.axis_size("lat")
    freqs_here, _, shot_total, lateral_width = surface.shape
    tile_rows, slots = tile_ids.shape[1:]
    blocks = pool.shape[2]
    levels = depth_size
    entries = tile_rows * lat_size
    shots_own = shot_total // lat_size
    shots_half = shots_own // 2
    swap = [(0, 1), (1, 0)]
    theirs = lax.dynamic_index_in_dim(pool[0], 2 * (1 - depth_index), 0, keepdims=False)
    remote_own = lax.ppermute(theirs, "depth", swap)
    remote_half = lax.ppermute(pool[0, 1], "depth", swap)
    lists = jnp.concatenate([tile_ids[0], block_ids[0], counts[0][:, None]], axis=1).astype(jnp.float32)
    lists = jnp.pad(lists, ((0, 0), (0, TILE - lists.shape[1])))
    tables = jnp.concatenate([refl.reshape(tile_rows, TILE), lists], axis=0)[None]
    tables = lax.all_gather(tables, "depth", axis=0, tiled=True)
    depth_id = depth_index.astype(jnp.int32).reshape(1)
    rows = tile_rows * (shots_own + shots_half + 2)
    packed = pl.pallas_call(
        functools.partial(pack_kernel, lat_size),
        out_shape=jax.ShapeDtypeStruct((lat_size, rows, 2 * TILE), jnp.bfloat16),
        in_specs=[pl.BlockSpec(memory_space=pltpu.SMEM), ANY_SPACE, VMEM_SPACE],
        out_specs=VMEM_SPACE,
        scratch_shapes=[
            pltpu.VMEM((2, shot_total, lateral_width), jnp.bfloat16),
            pltpu.VMEM((2, shot_total // 2, lateral_width), jnp.bfloat16),
            pltpu.SemaphoreType.DMA((2,)),
        ],
        name="pack",
    )(depth_id, surface, tables)
    wave = lax.all_to_all(packed, "lat", 0, 0, tiled=True)
    listed = wave[:, rows - tile_rows:, TILE:].reshape(entries, TILE).astype(jnp.int32)
    listed = jnp.stack([listed[:, :HALF], listed[:, HALF:]], 0)
    live_count = listed[:, :, 2 * slots]
    index = listed[:, :, slots:2 * slots] * entries + listed[:, :, :slots]
    live = jnp.arange(slots)[None, None, :] < live_count[:, :, None]
    index = jnp.where(live, index, blocks * entries)
    scale = 1.0 / jnp.sqrt(live_count.astype(jnp.float32))
    own_freq = 2 * depth_id
    half_freq = jnp.ones((1,), jnp.int32)
    image = jnp.zeros((levels * entries, TILE), jnp.float32)
    image = run_levels(
        shots_own, 0, index, scale, wave, pool, remote_own, image, depth_id, own_freq
    )
    image = run_levels(
        shots_half, tile_rows * shots_own, index, scale, wave, pool, remote_half, image, depth_id,
        half_freq,
    )
    freq_size = lax.axis_size("freq")
    spread = jnp.broadcast_to(
        image.reshape(levels, lat_size, 1, tile_rows, TILE),
        (levels, lat_size, freq_size, tile_rows, TILE),
    ).reshape(levels * lat_size * freq_size, tile_rows, TILE)
    parts = lax.all_to_all(spread, ("depth", "lat", "freq"), 0, 0, tiled=True)
    summed = jnp.sum(parts, axis=0).reshape(1, lateral_width)
    passing = 1.0 - refl
    factor = jnp.where(depth_index == levels - 1, passing * passing, 1.0)
    return summed * factor / (freqs_here * freq_size * shot_total)


def fits_fast(mesh, surface, pool, tile_ids):
    depth, lat, freq = (mesh.shape[name] for name in ("depth", "lat", "freq"))
    freqs, _, shots, width = surface.shape
    return (
        depth == 2
        and pool.shape[0] == depth
        and freqs == 3 * freq
        and shots == 16 * lat
        and tile_ids.shape[1] * TILE == width
        and tile_ids.shape[1] == 8 * lat
        and 2 * tile_ids.shape[2] < HALF
        and max(tile_ids.shape[1], pool.shape[2]) <= 256
    )


def solution(mesh):
    placed = (
        P("freq", None, None, "lat"),
        P("depth", "lat"),
        P("depth", "freq", None, None, None),
        P("depth", "lat", None),
        P("depth", "lat", None),
        P("depth", "lat"),
    )

    def whole(surface, refl, pool, tile_ids, block_ids, counts):
        fast = fits_fast(mesh, surface, pool, tile_ids)
        mapped = jax.shard_map(
            per_device_fast if fast else per_device, mesh=mesh, in_specs=placed,
            out_specs=P("depth", "lat"), check_vma=False,
        )
        return mapped(surface, refl, pool, tile_ids, block_ids, counts)

    return whole
```

```python
import functools

import jax
import jax.numpy as jnp
from jax import lax
from jax.experimental import pallas as pl
from jax.experimental.pallas import tpu as pltpu
from jax.sharding import PartitionSpec as P

TILE = 128
TILE_DEV = 8


def extended_2(block, sides, width):
    for axis, dim in sides:
        count = lax.axis_size(axis)
        forward = [(i, i + 1) for i in range(count - 1)]
        forward.append((count - 1, 0))
        backward = [(target, source) for source, target in forward]
        low = lax.ppermute(
            lax.slice_in_dim(block, block.shape[dim] - width, None, axis=dim), axis, forward
        )
        high = lax.ppermute(lax.slice_in_dim(block, 0, width, axis=dim), axis, backward)
        block = jnp.concatenate([low, block, high], axis=dim)
    return block


def aperture_rim(wave_field):
    return extended_2(wave_field, (("lat", 3),), TILE_DEV * TILE)


def extrapolate(extended, pool_level, local_ids, block_level, count_level, refl_level):
    freqs_here = extended.shape[0]
    shot_rows = extended.shape[2]
    tile_rows = local_ids.shape[0]
    slot_total = local_ids.shape[1]
    tile_grid = extended.reshape(freqs_here, 2, shot_rows, -1, TILE)
    slot_live = (jnp.arange(slot_total)[None, :] < count_level[:, None]).astype(jnp.bfloat16)
    picked = jnp.take(tile_grid, local_ids, axis=3) * slot_live[None, None, None, :, :, None]
    chosen = jnp.take(pool_level, block_level, axis=1)
    product = jnp.einsum("fsarkt,frktc->rfsac", picked, chosen, preferred_element_type=jnp.float32)
    real_part = product[:, :, 0, :, :TILE] - product[:, :, 1, :, TILE:]
    imag_part = product[:, :, 0, :, TILE:] + product[:, :, 1, :, :TILE]
    row_scale = 1.0 / jnp.sqrt(count_level.astype(jnp.float32))
    rows_out = jnp.stack([real_part, imag_part], 2) * row_scale[:, None, None, None, None]
    wave_out = jnp.transpose(rows_out, (1, 2, 3, 0, 4)).reshape(
        freqs_here, 2, shot_rows, tile_rows * TILE
    )
    wave_out = wave_out * (1.0 - refl_level)
    return (wave_out.astype(jnp.bfloat16), jnp.sum(wave_out * wave_out, axis=(0, 1, 2)))


def per_device(surface, refl, pool, tile_ids, block_ids, counts):
    depth_index = lax.axis_index("depth")
    lat_index = lax.axis_index("lat")
    tile_count = TILE_DEV * lax.axis_size("lat")
    first_tile = lat_index * TILE_DEV - TILE_DEV
    freqs_here = surface.shape[0]
    shot_total = surface.shape[2]
    lateral_width = surface.shape[3]
    shot_rows = shot_total // lax.axis_size("depth")
    own_shots = lax.dynamic_slice_in_dim(surface, depth_index * shot_rows, shot_rows, 2)
    pool_all = lax.all_gather(pool, "depth", axis=0, tiled=True)
    ids_all, blocks_all, counts_all = (
        lax.all_gather(tile_ids, "depth", axis=0, tiled=True),
        lax.all_gather(block_ids, "depth", axis=0, tiled=True),
        lax.all_gather(counts, "depth", axis=0, tiled=True),
    )
    refl_all = lax.all_gather(refl, "depth", axis=0, tiled=True)
    level_total = pool_all.shape[0]

    def level_step(level_index, loop_state):
        wave_field, images = loop_state
        ids_here = lax.dynamic_index_in_dim(ids_all, level_index, 0, keepdims=False)
        local_level = jnp.mod(ids_here - first_tile, tile_count)
        pool_here = lax.dynamic_index_in_dim(pool_all, level_index, 0, keepdims=False)
        blocks_here = lax.dynamic_index_in_dim(blocks_all, level_index, 0, keepdims=False)
        counts_here = lax.dynamic_index_in_dim(counts_all, level_index, 0, keepdims=False)
        refl_here = lax.dynamic_index_in_dim(refl_all, level_index, 0, keepdims=False)
        handed, partial_value = extrapolate(
            aperture_rim(wave_field), pool_here, local_level, blocks_here, counts_here, refl_here
        )
        images = lax.dynamic_update_index_in_dim(images, partial_value, level_index, 0)
        return (handed, images)

    start_images = jnp.zeros((level_total, lateral_width), jnp.float32)
    loop_state = lax.fori_loop(0, level_total, level_step, (own_shots, start_images))
    image_local = lax.psum_scatter(loop_state[1], "depth", scatter_dimension=0, tiled=True)[0]
    summed = lax.psum(image_local, "freq")
    divisor = freqs_here * lax.axis_size("freq") * shot_total
    return (summed / divisor)[None, :]


ROWS_STEP = 4
LANES = 128
HALF = LANES // 2
SUBLANES = 8
PACKED = 16
VMEM_SPACE = pl.BlockSpec(memory_space=pltpu.VMEM)
SMEM_SPACE = pl.BlockSpec(memory_space=pltpu.SMEM)
ANY_SPACE = pl.BlockSpec(memory_space=pl.ANY)


def table_kernel(refl_ref, tiles_ref, blocks_ref, counts_ref, out_ref):
    rows = tiles_ref.shape[1]
    slots = tiles_ref.shape[2]
    for row in range(rows):
        out_ref[row:row + 1, :] = refl_ref[:, row * LANES:(row + 1) * LANES]
    out_ref[rows:, :] = jnp.zeros((rows, LANES), jnp.float32)
    out_ref[rows:, :slots] = blocks_ref[0].astype(jnp.float32)
    out_ref[rows:, slots:2 * slots] = tiles_ref[0].astype(jnp.float32)
    spread = jnp.broadcast_to(counts_ref[...].astype(jnp.float32), (rows, rows))
    across = lax.broadcasted_iota(jnp.int32, (rows, rows), 1)
    down = lax.broadcasted_iota(jnp.int32, (rows, rows), 0)
    column = jnp.sum(jnp.where(across == down, spread, 0.0), axis=1, keepdims=True)
    out_ref[rows:, 2 * slots:2 * slots + 1] = column


def pack_kernel(depth_ref, lat_ref, surface_ref, mine_ref, other_ref, *refs):
    outs, sems = refs[:-1], refs[-1]
    lat_size = len(outs)
    depth_index = depth_ref[0]
    shot_total = surface_ref.shape[2]
    own = shot_total // lat_size
    half = own // 2
    copies = []
    for turn in range(lat_size):
        target = lax.rem(lat_ref[0] + turn, lat_size)
        own_start = pl.multiple_of(target * own, own)
        half_start = pl.multiple_of(depth_index * (shot_total // 2) + target * half, half)
        for part in range(2):
            copies.append(
                pltpu.make_async_copy(
                    surface_ref.at[2 * depth_index, part, pl.ds(own_start, own), :],
                    outs[turn].at[pl.ds(part * own, own), :],
                    sems.at[turn, 2 * part],
                )
            )
            copies.append(
                pltpu.make_async_copy(
                    surface_ref.at[1, part, pl.ds(half_start, half), :],
                    outs[turn].at[pl.ds(2 * own + part * half, half), :],
                    sems.at[turn, 2 * part + 1],
                )
            )
    for copy in copies:
        copy.start()
    rows = mine_ref.shape[0] // 2
    first = jnp.where(depth_index == 0, mine_ref[...], other_ref[...])
    second = jnp.where(depth_index == 0, other_ref[rows:, :], mine_ref[rows:, :])
    refl = first[:rows]
    high = refl.astype(jnp.bfloat16).astype(jnp.float32)
    rest = refl - high
    middle = rest.astype(jnp.bfloat16).astype(jnp.float32)
    low = rest - middle
    lists = first[rows:] + pltpu.roll(second, HALF, 1)
    line = jnp.concatenate([high, middle, low, lists], axis=1).astype(jnp.bfloat16)
    for out in outs:
        out[2 * own + 2 * half:, :4 * LANES] = line
    for copy in copies:
        copy.wait()


def level_kernel(lat_size, freq_size, slots, levels, depth_ref, lat_ref, *refs):
    waves = refs[:lat_size]
    (local_ref, remote_own_ref, remote_half_ref, image_ref, pool_own, pool_half, table, own_buf,
     half_buf, squares_buf, lists_buf, factor_buf, index_buf, index_ref, sems) = refs[lat_size:]
    blocks = pool_own.shape[1]
    entries = lists_buf.shape[0]
    rows = entries // lat_size
    own = own_buf.shape[0] // entries
    half = own // 2
    unit = 2 * (own + half)
    depth_index = depth_ref[0]
    copies = [
        pltpu.make_async_copy(local_ref.at[0, 2 * depth_index], pool_own.at[depth_index], sems.at[0]),
        pltpu.make_async_copy(remote_own_ref, pool_own.at[1 - depth_index], sems.at[1]),
        pltpu.make_async_copy(local_ref.at[0, 1], pool_half.at[depth_index], sems.at[2]),
        pltpu.make_async_copy(remote_half_ref, pool_half.at[1 - depth_index], sems.at[3]),
    ]
    for copy in copies:
        copy.start()

    base = 2 * (own + half)
    for turn, wave in enumerate(waves):
        source = lax.rem(lat_ref[0] + lat_size - turn, lat_size)
        line = wave[base:base + rows, :4 * LANES].astype(jnp.float32)
        refl = (line[:, :LANES] + line[:, LANES:2 * LANES]) + line[:, 2 * LANES:3 * LANES]
        start = pl.multiple_of(source * rows, rows)
        factor_buf[0, pl.ds(start, rows), :] = 1.0 - refl
        lists_buf[pl.ds(start, rows), :] = line[:, 3 * LANES:]
    lane = lax.broadcasted_iota(jnp.int32, (entries, LANES), 1)
    for level in range(levels):
        listed = lists_buf[...] if level == 0 else pltpu.roll(lists_buf[...], LANES - HALF, 1)
        count = jnp.broadcast_to(listed[:, 2 * slots:2 * slots + 1], (entries, LANES))
        tile = pltpu.roll(listed, LANES - slots, 1)
        live = lane.astype(jnp.float32) < count
        place = jnp.where(live, listed * entries + tile, float(blocks * entries))
        index_buf[level] = (place * unit).astype(jnp.int32)
        scale = 1.0 / jnp.sqrt(count)
        if level == 0:
            factor_buf[0] = factor_buf[0] * scale
        else:
            factor_buf[level] = scale
    index_copy = pltpu.make_async_copy(index_buf, index_ref, sems.at[4])
    index_copy.start()
    table[blocks * entries * unit:, :] = jnp.zeros((unit, LANES), jnp.float32)

    for turn, wave in enumerate(waves):
        source = lax.rem(lat_ref[0] + lat_size - turn, lat_size)
        for tile in range(rows):
            lanes = slice(tile * LANES, (tile + 1) * LANES)
            start = pl.multiple_of((source * rows + tile) * own, own)
            own_buf[pl.ds(start, own), :] = jnp.concatenate(
                [wave[:own, lanes], wave[own:2 * own, lanes]], axis=1
            )
        for tile in range(0, rows, 2):
            parts = []
            for part in range(2):
                span = slice(2 * own + part * half, 2 * own + (part + 1) * half)
                pieces = [
                    wave[span, (tile + k) * LANES:(tile + k + 1) * LANES].astype(jnp.float32)
                    for k in range(2)
                ]
                parts.append(jnp.concatenate(pieces, axis=0).astype(jnp.bfloat16))
            start = pl.multiple_of((source * rows + tile) * half, 2 * half)
            half_buf[pl.ds(start, 2 * half), :] = jnp.concatenate(parts, axis=1)
    for copy in copies:
        copy.wait()

    chunk = entries // 2

    def weights_of(upper):
        lower = jnp.concatenate([-upper[:, TILE:], upper[:, :TILE]], axis=1)
        return jnp.concatenate([upper, lower], axis=0)

    def halves(product, shots):
        product = product.reshape(chunk, shots, 2 * TILE)
        return [product[:, :, :TILE], product[:, :, TILE:]]

    for level in range(levels):
        last = level == levels - 1

        def block_step(block, carry):
            weights_own = weights_of(pool_own[level, block])
            weights_half = weights_of(pool_half[level, block])
            for step in range(2):
                span_own = slice(step * chunk * own, (step + 1) * chunk * own)
                span_half = slice(step * chunk * half, (step + 1) * chunk * half)
                product_own = jnp.dot(
                    own_buf[span_own, :], weights_own, preferred_element_type=jnp.float32
                )
                product_half = jnp.dot(
                    half_buf[span_half, :], weights_half, preferred_element_type=jnp.float32
                )
                joined = jnp.concatenate(halves(product_own, own) + halves(product_half, half), axis=1)
                start = pl.multiple_of((block * 2 + step) * chunk * unit, chunk * unit)
                table[pl.ds(start, chunk * unit), :] = joined.reshape(chunk * unit, LANES)
            return carry

        lax.fori_loop(0, blocks, block_step, 0)
        if level == 0:
            index_copy.wait()

        def row_step(step, carry):
            outs = []
            for inner in range(ROWS_STEP):
                row = step * ROWS_STEP + inner
                total = None
                for slot in range(slots):
                    start = pl.multiple_of(index_ref[level, row, slot], SUBLANES)
                    term = table[pl.ds(start, unit), :]
                    total = term if total is None else total + term
                total = total * factor_buf[level, pl.ds(row, 1), :]
                outs.append(total)
                squares = total * total
                squares_buf[level * entries + row] = jnp.sum(
                    squares.reshape(unit // SUBLANES, SUBLANES, LANES), axis=0
                )
            if not last:
                for k, out in enumerate(outs):
                    start = pl.multiple_of((step * ROWS_STEP + k) * own, own)
                    own_buf[pl.ds(start, own), :] = jnp.concatenate(
                        [out[:own], out[own:2 * own]], axis=1
                    ).astype(jnp.bfloat16)
                for k in range(0, ROWS_STEP, 2):
                    pair = outs[k:k + 2]
                    real = jnp.concatenate([out[2 * own:2 * own + half] for out in pair], axis=0)
                    imag = jnp.concatenate([out[2 * own + half:] for out in pair], axis=0)
                    start = pl.multiple_of((step * ROWS_STEP + k) * half, 2 * half)
                    half_buf[pl.ds(start, 2 * half), :] = jnp.concatenate(
                        [real, imag], axis=1
                    ).astype(jnp.bfloat16)
            return carry

        lax.fori_loop(0, entries // ROWS_STEP, row_step, 0)

    summed = jnp.sum(squares_buf[...], axis=1)
    for level in range(levels):
        for target in range(lat_size):
            start = level * entries + target * rows
            for copy in range(freq_size):
                image_ref[level, target, copy] = summed[start:start + rows]


def per_device_fast(surface, refl, pool, tile_ids, block_ids, counts):
    depth_index = lax.axis_index("depth")
    lat_index = lax.axis_index("lat")
    levels = lax.axis_size("depth")
    lat_size = lax.axis_size("lat")
    freq_size = lax.axis_size("freq")
    freqs_here, _, shot_total, lateral_width = surface.shape
    rows, slots = tile_ids.shape[1:]
    blocks = pool.shape[2]
    entries = rows * lat_size
    own = shot_total // lat_size
    half = own // 2
    height = 2 * (own + half) + rows
    swap = [(0, 1), (1, 0)]
    depth_id = depth_index.astype(jnp.int32).reshape(1)
    lat_id = lat_index.astype(jnp.int32).reshape(1)

    mine = pl.pallas_call(
        table_kernel,
        out_shape=jax.ShapeDtypeStruct((2 * rows, LANES), jnp.float32),
        in_specs=[VMEM_SPACE] * 4,
        out_specs=VMEM_SPACE,
        name="tables",
    )(refl, tile_ids, block_ids, counts)
    other = lax.ppermute(mine, "depth", swap)
    theirs = lax.dynamic_index_in_dim(pool[0], 2 * (1 - depth_index), 0, keepdims=False)
    remote_own = lax.ppermute(theirs, "depth", swap)
    remote_half = lax.ppermute(pool[0, 1], "depth", swap)

    chunks = pl.pallas_call(
        pack_kernel,
        out_shape=[jax.ShapeDtypeStruct((height, lateral_width), jnp.bfloat16)] * lat_size,
        in_specs=[SMEM_SPACE] * 2 + [ANY_SPACE] + [VMEM_SPACE] * 2,
        out_specs=[VMEM_SPACE] * lat_size,
        scratch_shapes=[pltpu.SemaphoreType.DMA((lat_size, 4))],
        name="pack",
    )(depth_id, lat_id, surface, mine, other)
    middle = lat_size // 2
    order = sorted(range(1, lat_size), key=lambda turn: abs(turn - middle))
    waves = [chunks[0]] + [None] * (lat_size - 1)
    for turn in order:
        around = [(source, (source + turn) % lat_size) for source in range(lat_size)]
        waves[turn] = lax.ppermute(chunks[turn], "lat", around)

    spread = pl.pallas_call(
        functools.partial(level_kernel, lat_size, freq_size, slots, levels),
        out_shape=jax.ShapeDtypeStruct((levels, lat_size, freq_size, rows, LANES), jnp.float32),
        in_specs=[SMEM_SPACE] * 2 + [VMEM_SPACE] * lat_size + [ANY_SPACE] * 3,
        out_specs=VMEM_SPACE,
        scratch_shapes=[
            pltpu.VMEM((levels, blocks, TILE, 2 * TILE), jnp.bfloat16),
            pltpu.VMEM((levels, blocks, TILE, 2 * TILE), jnp.bfloat16),
            pltpu.VMEM(((blocks * entries + 1) * 2 * (own + half), LANES), jnp.float32),
            pltpu.VMEM((entries * own, 2 * TILE), jnp.bfloat16),
            pltpu.VMEM((entries * half, 2 * TILE), jnp.bfloat16),
            pltpu.VMEM((levels * entries, SUBLANES, LANES), jnp.float32),
            pltpu.VMEM((entries, LANES), jnp.float32),
            pltpu.VMEM((levels, entries, LANES), jnp.float32),
            pltpu.VMEM((levels, entries, LANES), jnp.int32),
            pltpu.SMEM((levels, entries, LANES), jnp.int32),
            pltpu.SemaphoreType.DMA((5,)),
        ],
        cost_estimate=pl.CostEstimate(
            flops=8 * levels * blocks * entries * (own + half) * TILE * TILE,
            bytes_accessed=4 * entries * (own + half) * TILE + 16 * blocks * TILE * TILE,
            transcendentals=0,
        ),
        name="levels",
    )(depth_id, lat_id, *waves, pool, remote_own, remote_half)
    spread = spread.reshape(levels * lat_size * freq_size, rows, LANES)
    parts = lax.all_to_all(spread, ("depth", "lat", "freq"), 0, 0, tiled=True)
    summed = jnp.sum(parts, axis=0).reshape(1, lateral_width)
    kept = 1.0 - refl
    factor = jnp.where(depth_index == levels - 1, kept * kept, 1.0)
    return summed * factor / (freqs_here * freq_size * shot_total)


def fits_fast(mesh, surface, pool, tile_ids):
    depth, lat, freq = (mesh.shape[name] for name in ("depth", "lat", "freq"))
    freqs, _, shots, width = surface.shape
    rows, slots = tile_ids.shape[1:]
    return (
        depth == 2
        and pool.shape[0] == depth
        and freqs == 3 * freq
        and shots == PACKED * lat
        and TILE == LANES
        and rows * TILE == width
        and rows == SUBLANES * lat
        and 2 * slots < HALF
        and max(rows, pool.shape[2]) <= 256
    )


def solution(mesh):
    placed = (
        P("freq", None, None, "lat"),
        P("depth", "lat"),
        P("depth", "freq", None, None, None),
        P("depth", "lat", None),
        P("depth", "lat", None),
        P("depth", "lat"),
    )

    def whole(surface, refl, pool, tile_ids, block_ids, counts):
        fast = fits_fast(mesh, surface, pool, tile_ids)
        mapped = jax.shard_map(
            per_device_fast if fast else per_device, mesh=mesh, in_specs=placed,
            out_specs=P("depth", "lat"), check_vma=False,
        )
        return mapped(surface, refl, pool, tile_ids, block_ids, counts)

    return whole
```

```python
import functools

import jax
import jax.numpy as jnp
from jax import lax
from jax.experimental import pallas as pl
from jax.experimental.pallas import tpu as pltpu
from jax.sharding import PartitionSpec as P

TILE = 128
TILE_DEV = 8


def extended_2(block, sides, width):
    for axis, dim in sides:
        count = lax.axis_size(axis)
        forward = [(i, i + 1) for i in range(count - 1)]
        forward.append((count - 1, 0))
        backward = [(target, source) for source, target in forward]
        low = lax.ppermute(
            lax.slice_in_dim(block, block.shape[dim] - width, None, axis=dim), axis, forward
        )
        high = lax.ppermute(lax.slice_in_dim(block, 0, width, axis=dim), axis, backward)
        block = jnp.concatenate([low, block, high], axis=dim)
    return block


def aperture_rim(wave_field):
    return extended_2(wave_field, (("lat", 3),), TILE_DEV * TILE)


def extrapolate(extended, pool_level, local_ids, block_level, count_level, refl_level):
    freqs_here = extended.shape[0]
    shot_rows = extended.shape[2]
    tile_rows = local_ids.shape[0]
    slot_total = local_ids.shape[1]
    tile_grid = extended.reshape(freqs_here, 2, shot_rows, -1, TILE)
    slot_live = (jnp.arange(slot_total)[None, :] < count_level[:, None]).astype(jnp.bfloat16)
    picked = jnp.take(tile_grid, local_ids, axis=3) * slot_live[None, None, None, :, :, None]
    chosen = jnp.take(pool_level, block_level, axis=1)
    product = jnp.einsum("fsarkt,frktc->rfsac", picked, chosen, preferred_element_type=jnp.float32)
    real_part = product[:, :, 0, :, :TILE] - product[:, :, 1, :, TILE:]
    imag_part = product[:, :, 0, :, TILE:] + product[:, :, 1, :, :TILE]
    row_scale = 1.0 / jnp.sqrt(count_level.astype(jnp.float32))
    rows_out = jnp.stack([real_part, imag_part], 2) * row_scale[:, None, None, None, None]
    wave_out = jnp.transpose(rows_out, (1, 2, 3, 0, 4)).reshape(
        freqs_here, 2, shot_rows, tile_rows * TILE
    )
    wave_out = wave_out * (1.0 - refl_level)
    return (wave_out.astype(jnp.bfloat16), jnp.sum(wave_out * wave_out, axis=(0, 1, 2)))


def per_device(surface, refl, pool, tile_ids, block_ids, counts):
    depth_index = lax.axis_index("depth")
    lat_index = lax.axis_index("lat")
    tile_count = TILE_DEV * lax.axis_size("lat")
    first_tile = lat_index * TILE_DEV - TILE_DEV
    freqs_here = surface.shape[0]
    shot_total = surface.shape[2]
    lateral_width = surface.shape[3]
    shot_rows = shot_total // lax.axis_size("depth")
    own_shots = lax.dynamic_slice_in_dim(surface, depth_index * shot_rows, shot_rows, 2)
    pool_all = lax.all_gather(pool, "depth", axis=0, tiled=True)
    ids_all, blocks_all, counts_all = (
        lax.all_gather(tile_ids, "depth", axis=0, tiled=True),
        lax.all_gather(block_ids, "depth", axis=0, tiled=True),
        lax.all_gather(counts, "depth", axis=0, tiled=True),
    )
    refl_all = lax.all_gather(refl, "depth", axis=0, tiled=True)
    level_total = pool_all.shape[0]

    def level_step(level_index, loop_state):
        wave_field, images = loop_state
        ids_here = lax.dynamic_index_in_dim(ids_all, level_index, 0, keepdims=False)
        local_level = jnp.mod(ids_here - first_tile, tile_count)
        pool_here = lax.dynamic_index_in_dim(pool_all, level_index, 0, keepdims=False)
        blocks_here = lax.dynamic_index_in_dim(blocks_all, level_index, 0, keepdims=False)
        counts_here = lax.dynamic_index_in_dim(counts_all, level_index, 0, keepdims=False)
        refl_here = lax.dynamic_index_in_dim(refl_all, level_index, 0, keepdims=False)
        handed, partial_value = extrapolate(
            aperture_rim(wave_field), pool_here, local_level, blocks_here, counts_here, refl_here
        )
        images = lax.dynamic_update_index_in_dim(images, partial_value, level_index, 0)
        return (handed, images)

    start_images = jnp.zeros((level_total, lateral_width), jnp.float32)
    loop_state = lax.fori_loop(0, level_total, level_step, (own_shots, start_images))
    image_local = lax.psum_scatter(loop_state[1], "depth", scatter_dimension=0, tiled=True)[0]
    summed = lax.psum(image_local, "freq")
    divisor = freqs_here * lax.axis_size("freq") * shot_total
    return (summed / divisor)[None, :]


ROWS_STEP = 4
LANES = 128
SUBLANES = 8
PACKED = 16
VMEM_SPACE = pl.BlockSpec(memory_space=pltpu.VMEM)
SMEM_SPACE = pl.BlockSpec(memory_space=pltpu.SMEM)
ANY_SPACE = pl.BlockSpec(memory_space=pl.ANY)


def front_kernel(
    depth_ref, lat_ref, surface_ref, pool_ref, refl_ref, tiles_ref, blocks_ref, counts_ref, *refs
):
    outs, send_own, send_half, lists_ref, sems = refs[:-4], *refs[-4:]
    lat_size = len(outs)
    depth_index = depth_ref[0]
    shot_total = surface_ref.shape[2]
    own = shot_total // lat_size
    half = own // 2
    pools = [
        pltpu.make_async_copy(pool_ref.at[0, 2 * (1 - depth_index)], send_own, sems.at[lat_size, 0]),
        pltpu.make_async_copy(pool_ref.at[0, 1], send_half, sems.at[lat_size, 1]),
    ]
    copies = []
    for turn in range(lat_size):
        target = lax.rem(lat_ref[0] + turn, lat_size)
        own_start = pl.multiple_of(target * own, own)
        half_start = pl.multiple_of(depth_index * (shot_total // 2) + target * half, half)
        for part in range(2):
            copies.append(
                pltpu.make_async_copy(
                    surface_ref.at[2 * depth_index, part, pl.ds(own_start, own), :],
                    outs[turn].at[pl.ds(part * own, own), :],
                    sems.at[turn, 2 * part],
                )
            )
            copies.append(
                pltpu.make_async_copy(
                    surface_ref.at[1, part, pl.ds(half_start, half), :],
                    outs[turn].at[pl.ds(2 * own + part * half, half), :],
                    sems.at[turn, 2 * part + 1],
                )
            )
    for copy in pools + copies:
        copy.start()
    rows = tiles_ref.shape[1]
    slots = tiles_ref.shape[2]
    for row in range(rows):
        lists_ref[0, row:row + 1, :] = refl_ref[:, row * LANES:(row + 1) * LANES]
    lists_ref[0, rows:, :] = jnp.zeros((rows, LANES), jnp.float32)
    lists_ref[0, rows:, :slots] = blocks_ref[0].astype(jnp.float32)
    lists_ref[0, rows:, slots:2 * slots] = tiles_ref[0].astype(jnp.float32)
    spread = jnp.broadcast_to(counts_ref[...].astype(jnp.float32), (rows, rows))
    across = lax.broadcasted_iota(jnp.int32, (rows, rows), 1)
    down = lax.broadcasted_iota(jnp.int32, (rows, rows), 0)
    column = jnp.sum(jnp.where(across == down, spread, 0.0), axis=1, keepdims=True)
    lists_ref[0, rows:, 2 * slots:2 * slots + 1] = column
    lists = lists_ref[0]
    for target in range(1, lists_ref.shape[0]):
        lists_ref[target] = lists
    for copy in pools + copies:
        copy.wait()


def level_kernel(lat_size, freq_size, slots, levels, depth_ref, lat_ref, lists_ref, *refs):
    wave_refs = refs[:lat_size]
    (local_ref, remote_own_ref, remote_half_ref, image_ref, table, own_buf, half_buf, squares_buf,
     factor_buf, index_buf, index_ref, sem) = refs[lat_size:]
    blocks = remote_own_ref.shape[0]
    entries = factor_buf.shape[1]
    rows = entries // lat_size
    own = own_buf.shape[0] // entries
    half = own // 2
    unit = 2 * (own + half)
    depth_index = depth_ref[0]
    lane = lax.broadcasted_iota(jnp.int32, (entries, LANES), 1)
    for level in range(levels):
        sources = range(level * lat_size, (level + 1) * lat_size)
        listed = jnp.concatenate([lists_ref[source, rows:, :] for source in sources], axis=0)
        count = jnp.broadcast_to(listed[:, 2 * slots:2 * slots + 1], (entries, LANES))
        tile = pltpu.roll(listed, LANES - slots, 1)
        live = lane.astype(jnp.float32) < count
        place = jnp.where(live, listed * entries + tile, float(blocks * entries))
        index_buf[level] = (place * unit).astype(jnp.int32)
        scale = 1.0 / jnp.sqrt(count)
        if level < levels - 1:
            refl = jnp.concatenate([lists_ref[source, :rows, :] for source in sources], axis=0)
            scale = scale * (1.0 - refl)
        factor_buf[level] = scale
    index_copy = pltpu.make_async_copy(index_buf, index_ref, sem)
    index_copy.start()
    table[blocks * entries * unit:, :] = jnp.zeros((unit, LANES), jnp.float32)

    for turn in range(lat_size):
        wave = wave_refs[turn]
        source = lax.rem(lat_ref[0] + lat_size - turn, lat_size)
        for tile in range(rows):
            lanes = slice(tile * LANES, (tile + 1) * LANES)
            start = pl.multiple_of((source * rows + tile) * own, own)
            own_buf[pl.ds(start, own), :] = jnp.concatenate(
                [wave[:own, lanes], wave[own:2 * own, lanes]], axis=1
            )
        for tile in range(0, rows, 2):
            parts = []
            for part in range(2):
                span = slice(2 * own + part * half, 2 * own + (part + 1) * half)
                pieces = [
                    wave[span, (tile + k) * LANES:(tile + k + 1) * LANES].astype(jnp.float32)
                    for k in range(2)
                ]
                parts.append(jnp.concatenate(pieces, axis=0).astype(jnp.bfloat16))
            start = pl.multiple_of((source * rows + tile) * half, 2 * half)
            half_buf[pl.ds(start, 2 * half), :] = jnp.concatenate(parts, axis=1)

    chunk = entries // 2

    def weights_of(level, local, remote):
        upper = jnp.where(depth_index == level, local, remote)
        lower = jnp.concatenate([-upper[:, TILE:], upper[:, :TILE]], axis=1)
        return jnp.concatenate([upper, lower], axis=0)

    def halves(product, shots):
        product = product.reshape(chunk, shots, 2 * TILE)
        return [product[:, :, :TILE], product[:, :, TILE:]]

    for level in range(levels):
        last = level == levels - 1

        def block_step(block, carry):
            weights_own = weights_of(
                level, local_ref[0, 2 * depth_index, block], remote_own_ref[block]
            )
            weights_half = weights_of(level, local_ref[0, 1, block], remote_half_ref[block])
            for step in range(2):
                span_own = slice(step * chunk * own, (step + 1) * chunk * own)
                span_half = slice(step * chunk * half, (step + 1) * chunk * half)
                product_own = jnp.dot(
                    own_buf[span_own, :], weights_own, preferred_element_type=jnp.float32
                )
                product_half = jnp.dot(
                    half_buf[span_half, :], weights_half, preferred_element_type=jnp.float32
                )
                joined = jnp.concatenate(halves(product_own, own) + halves(product_half, half), axis=1)
                start = pl.multiple_of((block * 2 + step) * chunk * unit, chunk * unit)
                table[pl.ds(start, chunk * unit), :] = joined.reshape(chunk * unit, LANES)
            return carry

        lax.fori_loop(0, blocks, block_step, 0)
        if level == 0:
            index_copy.wait()

        def row_step(step, carry):
            outs = []
            for inner in range(ROWS_STEP):
                row = step * ROWS_STEP + inner
                total = None
                for slot in range(slots):
                    start = pl.multiple_of(index_ref[level, row, slot], SUBLANES)
                    term = table[pl.ds(start, unit), :]
                    total = term if total is None else total + term
                total = total * factor_buf[level, pl.ds(row, 1), :]
                outs.append(total)
                squares = total * total
                squares_buf[level * entries + row] = jnp.sum(
                    squares.reshape(unit // SUBLANES, SUBLANES, LANES), axis=0
                )
            if not last:
                for k, out in enumerate(outs):
                    start = pl.multiple_of((step * ROWS_STEP + k) * own, own)
                    own_buf[pl.ds(start, own), :] = jnp.concatenate(
                        [out[:own], out[own:2 * own]], axis=1
                    ).astype(jnp.bfloat16)
                for k in range(0, ROWS_STEP, 2):
                    pair = outs[k:k + 2]
                    real = jnp.concatenate([out[2 * own:2 * own + half] for out in pair], axis=0)
                    imag = jnp.concatenate([out[2 * own + half:] for out in pair], axis=0)
                    start = pl.multiple_of((step * ROWS_STEP + k) * half, 2 * half)
                    half_buf[pl.ds(start, 2 * half), :] = jnp.concatenate(
                        [real, imag], axis=1
                    ).astype(jnp.bfloat16)
            return carry

        lax.fori_loop(0, entries // ROWS_STEP, row_step, 0)

    summed = jnp.sum(squares_buf[...], axis=1)
    for level in range(levels):
        for target in range(lat_size):
            start = level * entries + target * rows
            for copy in range(freq_size):
                image_ref[level, target, copy] = summed[start:start + rows]


def per_device_fast(surface, refl, pool, tile_ids, block_ids, counts):
    depth_index = lax.axis_index("depth")
    lat_index = lax.axis_index("lat")
    levels = lax.axis_size("depth")
    lat_size = lax.axis_size("lat")
    freq_size = lax.axis_size("freq")
    freqs_here, _, shot_total, lateral_width = surface.shape
    rows, slots = tile_ids.shape[1:]
    blocks = pool.shape[2]
    entries = rows * lat_size
    own = shot_total // lat_size
    half = own // 2
    height = 2 * (own + half)
    swap = [(0, 1), (1, 0)]
    depth_id = depth_index.astype(jnp.int32).reshape(1)
    lat_id = lat_index.astype(jnp.int32).reshape(1)

    sent = jax.ShapeDtypeStruct(pool.shape[2:], pool.dtype)
    *chunks, send_own, send_half, lists = pl.pallas_call(
        front_kernel,
        out_shape=[jax.ShapeDtypeStruct((height, lateral_width), jnp.bfloat16)] * lat_size
        + [sent, sent, jax.ShapeDtypeStruct((levels * lat_size, 2 * rows, LANES), jnp.float32)],
        in_specs=[SMEM_SPACE] * 2 + [ANY_SPACE] * 2 + [VMEM_SPACE] * 4,
        out_specs=[VMEM_SPACE] * (lat_size + 3),
        scratch_shapes=[pltpu.SemaphoreType.DMA((lat_size + 1, 4))],
        name="front",
    )(depth_id, lat_id, surface, pool, refl, tile_ids, block_ids, counts)
    remote_own = lax.ppermute(send_own, "depth", swap)
    remote_half = lax.ppermute(send_half, "depth", swap)
    middle = lat_size // 2
    order = sorted(range(1, lat_size), key=lambda turn: abs(turn - middle))
    waves = [chunks[0]] + [None] * (lat_size - 1)
    for turn in order:
        around = [(source, (source + turn) % lat_size) for source in range(lat_size)]
        waves[turn] = lax.ppermute(chunks[turn], "lat", around)
    lists = lax.all_to_all(lists, ("depth", "lat"), 0, 0, tiled=True)

    spread = pl.pallas_call(
        functools.partial(level_kernel, lat_size, freq_size, slots, levels),
        out_shape=jax.ShapeDtypeStruct((levels, lat_size, freq_size, rows, LANES), jnp.float32),
        in_specs=[SMEM_SPACE] * 2 + [VMEM_SPACE] * (lat_size + 4),
        out_specs=VMEM_SPACE,
        scratch_shapes=[
            pltpu.VMEM(((blocks * entries + 1) * 2 * (own + half), LANES), jnp.float32),
            pltpu.VMEM((entries * own, 2 * TILE), jnp.bfloat16),
            pltpu.VMEM((entries * half, 2 * TILE), jnp.bfloat16),
            pltpu.VMEM((levels * entries, SUBLANES, LANES), jnp.float32),
            pltpu.VMEM((levels, entries, LANES), jnp.float32),
            pltpu.VMEM((levels, entries, LANES), jnp.int32),
            pltpu.SMEM((levels, entries, LANES), jnp.int32),
            pltpu.SemaphoreType.DMA,
        ],
        cost_estimate=pl.CostEstimate(
            flops=8 * levels * blocks * entries * (own + half) * TILE * TILE,
            bytes_accessed=4 * entries * (own + half) * TILE + 16 * blocks * TILE * TILE,
            transcendentals=0,
        ),
        compiler_params=pltpu.CompilerParams(vmem_limit_bytes=32 << 20),
        name="levels",
    )(depth_id, lat_id, lists, *waves, pool, remote_own, remote_half)
    spread = spread.reshape(levels * lat_size * freq_size, rows, LANES)
    parts = lax.all_to_all(spread, ("depth", "lat", "freq"), 0, 0, tiled=True)
    summed = jnp.sum(parts, axis=0).reshape(1, lateral_width)
    kept = 1.0 - refl
    factor = jnp.where(depth_index == levels - 1, kept * kept, 1.0)
    return summed * factor / (freqs_here * freq_size * shot_total)


def fits_fast(mesh, surface, pool, tile_ids):
    depth, lat, freq = (mesh.shape[name] for name in ("depth", "lat", "freq"))
    freqs, _, shots, width = surface.shape
    rows, slots = tile_ids.shape[1:]
    return (
        depth == 2
        and pool.shape[0] == depth
        and freqs == 3 * freq
        and shots == PACKED * lat
        and TILE == LANES
        and rows * TILE == width
        and rows == SUBLANES * lat
        and 2 * slots < LANES
    )


def solution(mesh):
    placed = (
        P("freq", None, None, "lat"),
        P("depth", "lat"),
        P("depth", "freq", None, None, None),
        P("depth", "lat", None),
        P("depth", "lat", None),
        P("depth", "lat"),
    )

    def whole(surface, refl, pool, tile_ids, block_ids, counts):
        fast = fits_fast(mesh, surface, pool, tile_ids)
        mapped = jax.shard_map(
            per_device_fast if fast else per_device, mesh=mesh, in_specs=placed,
            out_specs=P("depth", "lat"), check_vma=False,
        )
        return mapped(surface, refl, pool, tile_ids, block_ids, counts)

    return whole
```

```python
import functools

import jax
import jax.numpy as jnp
from jax import lax
from jax.experimental import pallas as pl
from jax.experimental.pallas import tpu as pltpu
from jax.sharding import PartitionSpec as P


TILE = 128
TILE_DEV = 8


def extended_2(block, sides, width):
    for axis, dim in sides:
        count = lax.axis_size(axis)
        forward = [(i, i + 1) for i in range(count - 1)]
        forward.append((count - 1, 0))
        backward = [(target, source) for source, target in forward]
        low = lax.ppermute(
            lax.slice_in_dim(block, block.shape[dim] - width, None, axis=dim), axis, forward
        )
        high = lax.ppermute(lax.slice_in_dim(block, 0, width, axis=dim), axis, backward)
        block = jnp.concatenate([low, block, high], axis=dim)
    return block


def aperture_rim(wave_field):
    return extended_2(wave_field, (("lat", 3),), TILE_DEV * TILE)


def extrapolate(extended, pool_level, local_ids, block_level, count_level, refl_level):
    freqs_here = extended.shape[0]
    shot_rows = extended.shape[2]
    tile_rows = local_ids.shape[0]
    slot_total = local_ids.shape[1]
    tile_grid = extended.reshape(freqs_here, 2, shot_rows, -1, TILE)
    slot_live = (jnp.arange(slot_total)[None, :] < count_level[:, None]).astype(jnp.bfloat16)
    picked = jnp.take(tile_grid, local_ids, axis=3) * slot_live[None, None, None, :, :, None]
    chosen = jnp.take(pool_level, block_level, axis=1)
    product = jnp.einsum("fsarkt,frktc->rfsac", picked, chosen, preferred_element_type=jnp.float32)
    real_part = product[:, :, 0, :, :TILE] - product[:, :, 1, :, TILE:]
    imag_part = product[:, :, 0, :, TILE:] + product[:, :, 1, :, :TILE]
    row_scale = 1.0 / jnp.sqrt(count_level.astype(jnp.float32))
    rows_out = jnp.stack([real_part, imag_part], 2) * row_scale[:, None, None, None, None]
    wave_out = jnp.transpose(rows_out, (1, 2, 3, 0, 4)).reshape(
        freqs_here, 2, shot_rows, tile_rows * TILE
    )
    wave_out = wave_out * (1.0 - refl_level)
    return (wave_out.astype(jnp.bfloat16), jnp.sum(wave_out * wave_out, axis=(0, 1, 2)))


def per_device(surface, refl, pool, tile_ids, block_ids, counts):
    depth_index = lax.axis_index("depth")
    lat_index = lax.axis_index("lat")
    tile_count = TILE_DEV * lax.axis_size("lat")
    first_tile = lat_index * TILE_DEV - TILE_DEV
    freqs_here = surface.shape[0]
    shot_total = surface.shape[2]
    lateral_width = surface.shape[3]
    shot_rows = shot_total // lax.axis_size("depth")
    own_shots = lax.dynamic_slice_in_dim(surface, depth_index * shot_rows, shot_rows, 2)
    pool_all = lax.all_gather(pool, "depth", axis=0, tiled=True)
    ids_all, blocks_all, counts_all = (
        lax.all_gather(tile_ids, "depth", axis=0, tiled=True),
        lax.all_gather(block_ids, "depth", axis=0, tiled=True),
        lax.all_gather(counts, "depth", axis=0, tiled=True),
    )
    refl_all = lax.all_gather(refl, "depth", axis=0, tiled=True)
    level_total = pool_all.shape[0]

    def level_step(level_index, loop_state):
        wave_field, images = loop_state
        ids_here = lax.dynamic_index_in_dim(ids_all, level_index, 0, keepdims=False)
        local_level = jnp.mod(ids_here - first_tile, tile_count)
        pool_here = lax.dynamic_index_in_dim(pool_all, level_index, 0, keepdims=False)
        blocks_here = lax.dynamic_index_in_dim(blocks_all, level_index, 0, keepdims=False)
        counts_here = lax.dynamic_index_in_dim(counts_all, level_index, 0, keepdims=False)
        refl_here = lax.dynamic_index_in_dim(refl_all, level_index, 0, keepdims=False)
        handed, partial_value = extrapolate(
            aperture_rim(wave_field), pool_here, local_level, blocks_here, counts_here, refl_here
        )
        images = lax.dynamic_update_index_in_dim(images, partial_value, level_index, 0)
        return (handed, images)

    start_images = jnp.zeros((level_total, lateral_width), jnp.float32)
    loop_state = lax.fori_loop(0, level_total, level_step, (own_shots, start_images))
    image_local = lax.psum_scatter(loop_state[1], "depth", scatter_dimension=0, tiled=True)[0]
    summed = lax.psum(image_local, "freq")
    divisor = freqs_here * lax.axis_size("freq") * shot_total
    return (summed / divisor)[None, :]


ROWS_STEP = 4
LANES = 128
SUBLANES = 8
PACKED = 16
VMEM_SPACE = pl.BlockSpec(memory_space=pltpu.VMEM)
SMEM_SPACE = pl.BlockSpec(memory_space=pltpu.SMEM)
ANY_SPACE = pl.BlockSpec(memory_space=pl.ANY)


def chunk_copies(surface_ref, depth_index, target, lat_size, out, sems):
    shot_total = surface_ref.shape[2]
    own = shot_total // lat_size
    half = own // 2
    own_start = pl.multiple_of(target * own, own)
    half_start = pl.multiple_of(depth_index * (shot_total // 2) + target * half, half)
    copies = []
    for part in range(2):
        copies.append(
            pltpu.make_async_copy(
                surface_ref.at[2 * depth_index, part, pl.ds(own_start, own), :],
                out.at[pl.ds(part * own, own), :],
                sems.at[2 * part],
            )
        )
        copies.append(
            pltpu.make_async_copy(
                surface_ref.at[1, part, pl.ds(half_start, half), :],
                out.at[pl.ds(2 * own + part * half, half), :],
                sems.at[2 * part + 1],
            )
        )
    return copies


def front_kernel(
    depth_ref, lat_ref, surface_ref, pool_ref, refl_ref, tiles_ref, blocks_ref, counts_ref, *refs
):
    outs, send_own, send_half, lists_ref, sems = refs[:-4], *refs[-4:]
    lat_size = len(outs) + 1
    depth_index = depth_ref[0]
    pools = [
        pltpu.make_async_copy(pool_ref.at[0, 2 * (1 - depth_index)], send_own, sems.at[0, 0]),
        pltpu.make_async_copy(pool_ref.at[0, 1], send_half, sems.at[0, 1]),
    ]
    copies = []
    for turn, out in enumerate(outs, 1):
        target = lax.rem(lat_ref[0] + turn, lat_size)
        copies += chunk_copies(surface_ref, depth_index, target, lat_size, out, sems.at[turn])
    for copy in pools + copies:
        copy.start()
    rows = tiles_ref.shape[1]
    slots = tiles_ref.shape[2]
    for row in range(rows):
        lists_ref[0, row:row + 1, :] = refl_ref[:, row * LANES:(row + 1) * LANES]
    lists_ref[0, rows:, :] = jnp.zeros((rows, LANES), jnp.float32)
    lists_ref[0, rows:, :slots] = blocks_ref[0].astype(jnp.float32)
    lists_ref[0, rows:, slots:2 * slots] = tiles_ref[0].astype(jnp.float32)
    spread = jnp.broadcast_to(counts_ref[...].astype(jnp.float32), (rows, rows))
    across = lax.broadcasted_iota(jnp.int32, (rows, rows), 1)
    down = lax.broadcasted_iota(jnp.int32, (rows, rows), 0)
    column = jnp.sum(jnp.where(across == down, spread, 0.0), axis=1, keepdims=True)
    lists_ref[0, rows:, 2 * slots:2 * slots + 1] = column
    lists = lists_ref[0]
    for target in range(1, lists_ref.shape[0]):
        lists_ref[target] = lists
    for copy in pools + copies:
        copy.wait()


def level_kernel(lat_size, freq_size, slots, levels, depth_ref, lat_ref, lists_ref, *refs):
    wave_refs = refs[:lat_size]
    (local_ref, remote_own_ref, remote_half_ref, image_ref, table, own_buf, half_buf, squares_buf,
     factor_buf, index_buf, mine, index_ref, sems) = refs[lat_size:]
    mine_copies = chunk_copies(
        wave_refs[0], depth_ref[0], lat_ref[0], lat_size, mine, sems.at[pl.ds(1, 4)]
    )
    for copy in mine_copies:
        copy.start()
    blocks = remote_own_ref.shape[0]
    entries = factor_buf.shape[1]
    rows = entries // lat_size
    own = own_buf.shape[0] // entries
    half = own // 2
    unit = 2 * (own + half)
    depth_index = depth_ref[0]
    lane = lax.broadcasted_iota(jnp.int32, (entries, LANES), 1)
    for level in range(levels):
        sources = range(level * lat_size, (level + 1) * lat_size)
        listed = jnp.concatenate([lists_ref[source, rows:, :] for source in sources], axis=0)
        count = jnp.broadcast_to(listed[:, 2 * slots:2 * slots + 1], (entries, LANES))
        tile = pltpu.roll(listed, LANES - slots, 1)
        live = lane.astype(jnp.float32) < count
        place = jnp.where(live, listed * entries + tile, float(blocks * entries))
        index_buf[level] = (place * unit).astype(jnp.int32)
        scale = 1.0 / jnp.sqrt(count)
        if level < levels - 1:
            refl = jnp.concatenate([lists_ref[source, :rows, :] for source in sources], axis=0)
            scale = scale * (1.0 - refl)
        factor_buf[level] = scale
    index_copy = pltpu.make_async_copy(index_buf, index_ref, sems.at[0])
    index_copy.start()
    table[blocks * entries * unit:, :] = jnp.zeros((unit, LANES), jnp.float32)

    for turn in list(range(1, lat_size)) + [0]:
        if turn == 0:
            for copy in mine_copies:
                copy.wait()
        wave = wave_refs[turn] if turn else mine
        source = lax.rem(lat_ref[0] + lat_size - turn, lat_size)
        for tile in range(rows):
            lanes = slice(tile * LANES, (tile + 1) * LANES)
            start = pl.multiple_of((source * rows + tile) * own, own)
            own_buf[pl.ds(start, own), :] = jnp.concatenate(
                [wave[:own, lanes], wave[own:2 * own, lanes]], axis=1
            )
        for tile in range(0, rows, 2):
            parts = []
            for part in range(2):
                span = slice(2 * own + part * half, 2 * own + (part + 1) * half)
                pieces = [
                    wave[span, (tile + k) * LANES:(tile + k + 1) * LANES].astype(jnp.float32)
                    for k in range(2)
                ]
                parts.append(jnp.concatenate(pieces, axis=0).astype(jnp.bfloat16))
            start = pl.multiple_of((source * rows + tile) * half, 2 * half)
            half_buf[pl.ds(start, 2 * half), :] = jnp.concatenate(parts, axis=1)

    chunk = entries // 2

    def weights_of(level, local, remote):
        upper = jnp.where(depth_index == level, local, remote)
        lower = jnp.concatenate([-upper[:, TILE:], upper[:, :TILE]], axis=1)
        return jnp.concatenate([upper, lower], axis=0)

    def halves(product, shots):
        product = product.reshape(chunk, shots, 2 * TILE)
        return [product[:, :, :TILE], product[:, :, TILE:]]

    for level in range(levels):
        last = level == levels - 1

        def block_step(block, carry):
            weights_own = weights_of(
                level, local_ref[0, 2 * depth_index, block], remote_own_ref[block]
            )
            weights_half = weights_of(level, local_ref[0, 1, block], remote_half_ref[block])
            for step in range(2):
                span_own = slice(step * chunk * own, (step + 1) * chunk * own)
                span_half = slice(step * chunk * half, (step + 1) * chunk * half)
                product_own = jnp.dot(
                    own_buf[span_own, :], weights_own, preferred_element_type=jnp.float32
                )
                product_half = jnp.dot(
                    half_buf[span_half, :], weights_half, preferred_element_type=jnp.float32
                )
                joined = jnp.concatenate(halves(product_own, own) + halves(product_half, half), axis=1)
                start = pl.multiple_of((block * 2 + step) * chunk * unit, chunk * unit)
                table[pl.ds(start, chunk * unit), :] = joined.reshape(chunk * unit, LANES)
            return carry

        lax.fori_loop(0, blocks, block_step, 0)
        if level == 0:
            index_copy.wait()

        def row_step(step, carry):
            outs = []
            for inner in range(ROWS_STEP):
                row = step * ROWS_STEP + inner
                total = None
                for slot in range(slots):
                    start = pl.multiple_of(index_ref[level, row, slot], SUBLANES)
                    term = table[pl.ds(start, unit), :]
                    total = term if total is None else total + term
                total = total * factor_buf[level, pl.ds(row, 1), :]
                outs.append(total)
                squares = total * total
                squares_buf[level * entries + row] = jnp.sum(
                    squares.reshape(unit // SUBLANES, SUBLANES, LANES), axis=0
                )
            if not last:
                for k, out in enumerate(outs):
                    start = pl.multiple_of((step * ROWS_STEP + k) * own, own)
                    own_buf[pl.ds(start, own), :] = jnp.concatenate(
                        [out[:own], out[own:2 * own]], axis=1
                    ).astype(jnp.bfloat16)
                for k in range(0, ROWS_STEP, 2):
                    pair = outs[k:k + 2]
                    real = jnp.concatenate([out[2 * own:2 * own + half] for out in pair], axis=0)
                    imag = jnp.concatenate([out[2 * own + half:] for out in pair], axis=0)
                    start = pl.multiple_of((step * ROWS_STEP + k) * half, 2 * half)
                    half_buf[pl.ds(start, 2 * half), :] = jnp.concatenate(
                        [real, imag], axis=1
                    ).astype(jnp.bfloat16)
            return carry

        lax.fori_loop(0, entries // ROWS_STEP, row_step, 0)

    summed = jnp.sum(squares_buf[...], axis=1)
    for level in range(levels):
        for target in range(lat_size):
            start = level * entries + target * rows
            for copy in range(freq_size):
                image_ref[level, target, copy] = summed[start:start + rows]


def per_device_fast(surface, refl, pool, tile_ids, block_ids, counts):
    depth_index = lax.axis_index("depth")
    lat_index = lax.axis_index("lat")
    levels = lax.axis_size("depth")
    lat_size = lax.axis_size("lat")
    freq_size = lax.axis_size("freq")
    freqs_here, _, shot_total, lateral_width = surface.shape
    rows, slots = tile_ids.shape[1:]
    blocks = pool.shape[2]
    entries = rows * lat_size
    own = shot_total // lat_size
    half = own // 2
    height = 2 * (own + half)
    swap = [(0, 1), (1, 0)]
    depth_id = depth_index.astype(jnp.int32).reshape(1)
    lat_id = lat_index.astype(jnp.int32).reshape(1)

    sent = jax.ShapeDtypeStruct(pool.shape[2:], pool.dtype)
    *chunks, send_own, send_half, lists = pl.pallas_call(
        front_kernel,
        out_shape=[jax.ShapeDtypeStruct((height, lateral_width), jnp.bfloat16)] * (lat_size - 1)
        + [sent, sent, jax.ShapeDtypeStruct((levels * lat_size, 2 * rows, LANES), jnp.float32)],
        in_specs=[SMEM_SPACE] * 2 + [ANY_SPACE] * 2 + [VMEM_SPACE] * 4,
        out_specs=[VMEM_SPACE] * (lat_size + 2),
        scratch_shapes=[pltpu.SemaphoreType.DMA((lat_size, 4))],
        name="front",
    )(depth_id, lat_id, surface, pool, refl, tile_ids, block_ids, counts)
    remote_own = lax.ppermute(send_own, "depth", swap)
    remote_half = lax.ppermute(send_half, "depth", swap)
    middle = lat_size // 2
    order = sorted(range(1, lat_size), key=lambda turn: abs(turn - middle))
    waves = [surface] + [None] * (lat_size - 1)
    for turn in order:
        around = [(source, (source + turn) % lat_size) for source in range(lat_size)]
        waves[turn] = lax.ppermute(chunks[turn - 1], "lat", around)
    lists = lax.all_to_all(lists, ("depth", "lat"), 0, 0, tiled=True)

    spread = pl.pallas_call(
        functools.partial(level_kernel, lat_size, freq_size, slots, levels),
        out_shape=jax.ShapeDtypeStruct((levels, lat_size, freq_size, rows, LANES), jnp.float32),
        in_specs=[SMEM_SPACE] * 2 + [VMEM_SPACE, ANY_SPACE] + [VMEM_SPACE] * (lat_size + 2),
        out_specs=VMEM_SPACE,
        scratch_shapes=[
            pltpu.VMEM(((blocks * entries + 1) * 2 * (own + half), LANES), jnp.float32),
            pltpu.VMEM((entries * own, 2 * TILE), jnp.bfloat16),
            pltpu.VMEM((entries * half, 2 * TILE), jnp.bfloat16),
            pltpu.VMEM((levels * entries, SUBLANES, LANES), jnp.float32),
            pltpu.VMEM((levels, entries, LANES), jnp.float32),
            pltpu.VMEM((levels, entries, LANES), jnp.int32),
            pltpu.VMEM((height, lateral_width), jnp.bfloat16),
            pltpu.SMEM((levels, entries, LANES), jnp.int32),
            pltpu.SemaphoreType.DMA((5,)),
        ],
        cost_estimate=pl.CostEstimate(
            flops=8 * levels * blocks * entries * (own + half) * TILE * TILE,
            bytes_accessed=4 * entries * (own + half) * TILE + 16 * blocks * TILE * TILE,
            transcendentals=0,
        ),
        compiler_params=pltpu.CompilerParams(vmem_limit_bytes=32 << 20),
        name="levels",
    )(depth_id, lat_id, lists, *waves, pool, remote_own, remote_half)
    spread = spread.reshape(levels * lat_size * freq_size, rows, LANES)
    parts = lax.all_to_all(spread, ("depth", "lat", "freq"), 0, 0, tiled=True)
    summed = jnp.sum(parts, axis=0).reshape(1, lateral_width)
    kept = 1.0 - refl
    factor = jnp.where(depth_index == levels - 1, kept * kept, 1.0)
    return summed * factor / (freqs_here * freq_size * shot_total)


def fits_fast(mesh, surface, pool, tile_ids):
    depth, lat, freq = (mesh.shape[name] for name in ("depth", "lat", "freq"))
    freqs, _, shots, width = surface.shape
    rows, slots = tile_ids.shape[1:]
    return (
        depth == 2
        and pool.shape[0] == depth
        and freqs == 3 * freq
        and shots == PACKED * lat
        and TILE == LANES
        and rows * TILE == width
        and rows == SUBLANES * lat
        and 2 * slots < LANES
    )


def solution(mesh):
    placed = (
        P("freq", None, None, "lat"),
        P("depth", "lat"),
        P("depth", "freq", None, None, None),
        P("depth", "lat", None),
        P("depth", "lat", None),
        P("depth", "lat"),
    )

    def whole(surface, refl, pool, tile_ids, block_ids, counts):
        fast = fits_fast(mesh, surface, pool, tile_ids)
        mapped = jax.shard_map(
            per_device_fast if fast else per_device, mesh=mesh, in_specs=placed,
            out_specs=P("depth", "lat"), check_vma=False,
        )
        return mapped(surface, refl, pool, tile_ids, block_ids, counts)

    return whole
```

```python
import functools

import jax
import jax.numpy as jnp
from jax import lax
from jax.experimental import pallas as pl
from jax.experimental.pallas import tpu as pltpu
from jax.sharding import PartitionSpec as P


TILE = 128
TILE_DEV = 8


def extended_2(block, sides, width):
    for axis, dim in sides:
        count = lax.axis_size(axis)
        forward = [(i, i + 1) for i in range(count - 1)]
        forward.append((count - 1, 0))
        backward = [(target, source) for source, target in forward]
        low = lax.ppermute(
            lax.slice_in_dim(block, block.shape[dim] - width, None, axis=dim), axis, forward
        )
        high = lax.ppermute(lax.slice_in_dim(block, 0, width, axis=dim), axis, backward)
        block = jnp.concatenate([low, block, high], axis=dim)
    return block


def aperture_rim(wave_field):
    return extended_2(wave_field, (("lat", 3),), TILE_DEV * TILE)


def extrapolate(extended, pool_level, local_ids, block_level, count_level, refl_level):
    freqs_here = extended.shape[0]
    shot_rows = extended.shape[2]
    tile_rows = local_ids.shape[0]
    slot_total = local_ids.shape[1]
    tile_grid = extended.reshape(freqs_here, 2, shot_rows, -1, TILE)
    slot_live = (jnp.arange(slot_total)[None, :] < count_level[:, None]).astype(jnp.bfloat16)
    picked = jnp.take(tile_grid, local_ids, axis=3) * slot_live[None, None, None, :, :, None]
    chosen = jnp.take(pool_level, block_level, axis=1)
    product = jnp.einsum("fsarkt,frktc->rfsac", picked, chosen, preferred_element_type=jnp.float32)
    real_part = product[:, :, 0, :, :TILE] - product[:, :, 1, :, TILE:]
    imag_part = product[:, :, 0, :, TILE:] + product[:, :, 1, :, :TILE]
    row_scale = 1.0 / jnp.sqrt(count_level.astype(jnp.float32))
    rows_out = jnp.stack([real_part, imag_part], 2) * row_scale[:, None, None, None, None]
    wave_out = jnp.transpose(rows_out, (1, 2, 3, 0, 4)).reshape(
        freqs_here, 2, shot_rows, tile_rows * TILE
    )
    wave_out = wave_out * (1.0 - refl_level)
    return (wave_out.astype(jnp.bfloat16), jnp.sum(wave_out * wave_out, axis=(0, 1, 2)))


def per_device(surface, refl, pool, tile_ids, block_ids, counts):
    depth_index = lax.axis_index("depth")
    lat_index = lax.axis_index("lat")
    tile_count = TILE_DEV * lax.axis_size("lat")
    first_tile = lat_index * TILE_DEV - TILE_DEV
    freqs_here = surface.shape[0]
    shot_total = surface.shape[2]
    lateral_width = surface.shape[3]
    shot_rows = shot_total // lax.axis_size("depth")
    own_shots = lax.dynamic_slice_in_dim(surface, depth_index * shot_rows, shot_rows, 2)
    pool_all = lax.all_gather(pool, "depth", axis=0, tiled=True)
    ids_all, blocks_all, counts_all = (
        lax.all_gather(tile_ids, "depth", axis=0, tiled=True),
        lax.all_gather(block_ids, "depth", axis=0, tiled=True),
        lax.all_gather(counts, "depth", axis=0, tiled=True),
    )
    refl_all = lax.all_gather(refl, "depth", axis=0, tiled=True)
    level_total = pool_all.shape[0]

    def level_step(level_index, loop_state):
        wave_field, images = loop_state
        ids_here = lax.dynamic_index_in_dim(ids_all, level_index, 0, keepdims=False)
        local_level = jnp.mod(ids_here - first_tile, tile_count)
        pool_here = lax.dynamic_index_in_dim(pool_all, level_index, 0, keepdims=False)
        blocks_here = lax.dynamic_index_in_dim(blocks_all, level_index, 0, keepdims=False)
        counts_here = lax.dynamic_index_in_dim(counts_all, level_index, 0, keepdims=False)
        refl_here = lax.dynamic_index_in_dim(refl_all, level_index, 0, keepdims=False)
        handed, partial_value = extrapolate(
            aperture_rim(wave_field), pool_here, local_level, blocks_here, counts_here, refl_here
        )
        images = lax.dynamic_update_index_in_dim(images, partial_value, level_index, 0)
        return (handed, images)

    start_images = jnp.zeros((level_total, lateral_width), jnp.float32)
    loop_state = lax.fori_loop(0, level_total, level_step, (own_shots, start_images))
    image_local = lax.psum_scatter(loop_state[1], "depth", scatter_dimension=0, tiled=True)[0]
    summed = lax.psum(image_local, "freq")
    divisor = freqs_here * lax.axis_size("freq") * shot_total
    return (summed / divisor)[None, :]


ROWS_STEP = 4
LANES = 128
SUBLANES = 8
HALF = LANES // 2
PACKED = 16
VMEM_SPACE = pl.BlockSpec(memory_space=pltpu.VMEM)
SMEM_SPACE = pl.BlockSpec(memory_space=pltpu.SMEM)
ANY_SPACE = pl.BlockSpec(memory_space=pl.ANY)


def table_kernel(
    depth_ref, pool_ref, refl_ref, tiles_ref, blocks_ref, counts_ref, out_ref, own_ref, half_ref, sems
):
    copies = [
        pltpu.make_async_copy(pool_ref.at[0, 2 * (1 - depth_ref[0])], own_ref, sems.at[0]),
        pltpu.make_async_copy(pool_ref.at[0, 1], half_ref, sems.at[1]),
    ]
    for copy in copies:
        copy.start()
    rows = tiles_ref.shape[1]
    slots = tiles_ref.shape[2]
    for row in range(rows):
        out_ref[row:row + 1, :] = refl_ref[:, row * LANES:(row + 1) * LANES]
    out_ref[rows:, :] = jnp.zeros((rows, LANES), jnp.float32)
    out_ref[rows:, :slots] = blocks_ref[0].astype(jnp.float32)
    out_ref[rows:, slots:2 * slots] = tiles_ref[0].astype(jnp.float32)
    spread = jnp.broadcast_to(counts_ref[...].astype(jnp.float32), (rows, rows))
    across = lax.broadcasted_iota(jnp.int32, (rows, rows), 1)
    down = lax.broadcasted_iota(jnp.int32, (rows, rows), 0)
    column = jnp.sum(jnp.where(across == down, spread, 0.0), axis=1, keepdims=True)
    out_ref[rows:, 2 * slots:2 * slots + 1] = column
    for copy in copies:
        copy.wait()


def front_kernel(lat_size, depth_ref, lat_ref, surface_ref, mine_ref, other_ref, *refs):
    outs, sems = refs[:-1], refs[-1]
    depth_index = depth_ref[0]
    groups = surface_ref.shape[2] // lat_size
    height = surface_ref.shape[3]
    rows = height // SUBLANES
    copies = []
    for turn, out in enumerate(outs, 1):
        target = lax.rem(lat_ref[0] + turn, lat_size)
        sources = [
            surface_ref.at[2 * depth_index, part, groups * target + group]
            for part in range(2)
            for group in range(groups)
        ] + [surface_ref.at[1, part, depth_index * lat_size + target] for part in range(2)]
        copies += [
            pltpu.make_async_copy(
                source, out.at[pl.ds(place * height, height), :], sems.at[turn - 1, place]
            )
            for place, source in enumerate(sources)
        ]
    for copy in copies:
        copy.start()
    first = jnp.where(depth_index == 0, mine_ref[...], other_ref[...])
    second = jnp.where(depth_index == 0, other_ref[rows:, :], mine_ref[rows:, :])
    refl = first[:rows]
    high = refl.astype(jnp.bfloat16)
    low = (refl - high.astype(jnp.float32)).astype(jnp.bfloat16)
    lists = first[rows:] + pltpu.roll(second, HALF, 1)
    pair = jnp.concatenate([high.astype(jnp.float32), low.astype(jnp.float32)], axis=0)
    for out in outs:
        start = out.shape[0] - 3 * rows
        out[start:start + 2 * rows, :] = pair.astype(jnp.bfloat16)
        out[start + 2 * rows:, :] = lists.astype(jnp.bfloat16)
    for copy in copies:
        copy.wait()


def level_kernel(lat_size, freq_size, slots, levels, depth_ref, lat_ref, *refs):
    wave_refs = refs[:lat_size]
    (local_ref, remote_own_ref, remote_half_ref, image_ref, table, own_buf, half_buf, squares_buf,
     lists_buf, factor_buf, index_buf, index_ref, sem) = refs[lat_size:]
    blocks = remote_own_ref.shape[0]
    entries = factor_buf.shape[1]
    rows = entries // lat_size
    own = own_buf.shape[0] // entries
    half = own // 2
    unit = 2 * (own + half)
    depth_index = depth_ref[0]
    for turn, wave in enumerate(wave_refs):
        source = lax.rem(lat_ref[0] + lat_size - turn, lat_size)
        top = wave.shape[0] - 3 * rows
        pair = wave[top:top + 2 * rows, :].astype(jnp.float32)
        high, low = pair[:rows], pair[rows:]
        lists = wave[top + 2 * rows:, :].astype(jnp.float32)
        start = pl.multiple_of(source * rows, rows)
        factor_buf[0, pl.ds(start, rows), :] = 1.0 - (high + low)
        lists_buf[pl.ds(start, rows), :] = lists
    lane = lax.broadcasted_iota(jnp.int32, (entries, LANES), 1).astype(jnp.float32)
    for level in range(levels):
        listed = lists_buf[...]
        if level:
            listed = pltpu.roll(listed, LANES - HALF, 1)
        count = jnp.broadcast_to(listed[:, 2 * slots:2 * slots + 1], (entries, LANES))
        tile = pltpu.roll(listed, LANES - slots, 1)
        place = jnp.where(lane < count, listed * entries + tile, float(blocks * entries))
        index_buf[level] = (place * unit).astype(jnp.int32)
        scale = 1.0 / jnp.sqrt(count)
        factor_buf[level] = scale if level == levels - 1 else scale * factor_buf[level]
    index_copy = pltpu.make_async_copy(index_buf, index_ref, sem)
    index_copy.start()
    table[blocks * entries * unit:, :] = jnp.zeros((unit, LANES), jnp.float32)

    for turn, wave in enumerate(wave_refs):
        source = lax.rem(lat_ref[0] + lat_size - turn, lat_size)

        height = rows * SUBLANES
        for part in range(2):
            lanes = slice(part * LANES, (part + 1) * LANES)
            for group in range(2):
                start = pl.multiple_of((source * 2 + group) * height, height)
                place = (part * 2 + group) * height
                own_buf[pl.ds(start, height), lanes] = wave[place:place + height, :]
            start = pl.multiple_of(source * height, height)
            place = (4 + part) * height
            half_buf[pl.ds(start, height), lanes] = wave[place:place + height, :]

    def weights_of(level, local, remote):
        upper = jnp.where(depth_index == level, local, remote)
        lower = jnp.concatenate([-upper[:, TILE:], upper[:, :TILE]], axis=1)
        return jnp.concatenate([upper, lower], axis=0)

    def units(product, groups):
        sources = lat_size if groups else 1
        product = product.reshape(sources, max(groups, 1), entries // sources, -1, 2 * TILE)
        return [
            product[:, group, :, :, part * TILE:(part + 1) * TILE].reshape(entries, -1, TILE)
            for part in range(2)
            for group in range(max(groups, 1))
        ]

    for level in range(levels):
        last = level == levels - 1

        def block_step(block, carry):
            weights_own = weights_of(
                level, local_ref[0, 2 * depth_index, block], remote_own_ref[block]
            )
            weights_half = weights_of(level, local_ref[0, 1, block], remote_half_ref[block])
            product_own = jnp.dot(own_buf[...], weights_own, preferred_element_type=jnp.float32)
            product_half = jnp.dot(half_buf[...], weights_half, preferred_element_type=jnp.float32)
            joined = units(product_own, 0 if level else own // SUBLANES) + units(product_half, 0)
            start = pl.multiple_of(block * entries * unit, entries * unit)
            table[pl.ds(start, entries * unit), :] = jnp.concatenate(joined, axis=1).reshape(
                entries * unit, LANES
            )
            return carry

        lax.fori_loop(0, blocks, block_step, 0, unroll=4)
        if level == 0:
            index_copy.wait()

        def row_step(step, carry):
            outs = []
            for inner in range(ROWS_STEP):
                row = step * ROWS_STEP + inner
                total = None
                for slot in range(slots):
                    start = pl.multiple_of(index_ref[level, row, slot], SUBLANES)
                    term = table[pl.ds(start, unit), :]
                    total = term if total is None else total + term
                total = total * factor_buf[level, pl.ds(row, 1), :]
                outs.append(total)
                squares = total * total
                squares_buf[level * entries + row] = jnp.sum(
                    squares.reshape(unit // SUBLANES, SUBLANES, LANES), axis=0
                )
            if not last:
                for k, out in enumerate(outs):
                    start = pl.multiple_of((step * ROWS_STEP + k) * own, own)
                    own_buf[pl.ds(start, own), :] = jnp.concatenate(
                        [out[:own], out[own:2 * own]], axis=1
                    ).astype(jnp.bfloat16)
                for k in range(0, ROWS_STEP, 2):
                    pair = outs[k:k + 2]
                    real = jnp.concatenate([out[2 * own:2 * own + half] for out in pair], axis=0)
                    imag = jnp.concatenate([out[2 * own + half:] for out in pair], axis=0)
                    start = pl.multiple_of((step * ROWS_STEP + k) * half, 2 * half)
                    half_buf[pl.ds(start, 2 * half), :] = jnp.concatenate(
                        [real, imag], axis=1
                    ).astype(jnp.bfloat16)
            return carry

        lax.fori_loop(0, entries // ROWS_STEP, row_step, 0)

    summed = jnp.sum(squares_buf[...], axis=1)
    for level in range(levels):
        for target in range(lat_size):
            start = level * entries + target * rows
            for copy in range(freq_size):
                image_ref[level, target, copy] = summed[start:start + rows]


def per_device_fast(surface, refl, pool, tile_ids, block_ids, counts):
    depth_index = lax.axis_index("depth")
    lat_index = lax.axis_index("lat")
    levels = lax.axis_size("depth")
    lat_size = lax.axis_size("lat")
    freq_size = lax.axis_size("freq")
    freqs_here, _, shot_total, lateral_width = surface.shape
    rows, slots = tile_ids.shape[1:]
    blocks = pool.shape[2]
    entries = rows * lat_size
    own = shot_total // lat_size
    half = own // 2
    swap = [(0, 1), (1, 0)]
    depth_id = depth_index.astype(jnp.int32).reshape(1)
    lat_id = lat_index.astype(jnp.int32).reshape(1)

    sent = jax.ShapeDtypeStruct(pool.shape[2:], pool.dtype)
    mine, send_own, send_half = pl.pallas_call(
        table_kernel,
        out_shape=[jax.ShapeDtypeStruct((2 * rows, LANES), jnp.float32), sent, sent],
        in_specs=[SMEM_SPACE, ANY_SPACE] + [VMEM_SPACE] * 4,
        out_specs=[VMEM_SPACE] * 3,
        scratch_shapes=[pltpu.SemaphoreType.DMA((2,))],
        name="tables",
    )(depth_id, pool, refl, tile_ids, block_ids, counts)
    other = lax.ppermute(mine, "depth", swap)
    remote_own = lax.ppermute(send_own, "depth", swap)
    remote_half = lax.ppermute(send_half, "depth", swap)

    pieces = surface.reshape(
        freqs_here, 2, shot_total // SUBLANES, SUBLANES, rows, LANES
    ).transpose(0, 1, 2, 4, 3, 5).reshape(
        freqs_here, 2, shot_total // SUBLANES, rows * SUBLANES, LANES
    )
    height = (2 * (own + half) + 3) * rows
    chunks = pl.pallas_call(
        functools.partial(front_kernel, lat_size),
        out_shape=[jax.ShapeDtypeStruct((height, LANES), jnp.bfloat16)] * (lat_size - 1),
        in_specs=[SMEM_SPACE] * 2 + [ANY_SPACE] + [VMEM_SPACE] * 2,
        out_specs=[VMEM_SPACE] * (lat_size - 1),
        scratch_shapes=[pltpu.SemaphoreType.DMA((lat_size - 1, 2 * (own + half) // SUBLANES))],
        name="front",
    )(depth_id, lat_id, pieces, mine, other)
    own_pieces = lax.dynamic_slice(
        pieces, (2 * depth_index, 0, lat_index * (own // SUBLANES), 0, 0),
        (1, 2, own // SUBLANES, rows * SUBLANES, LANES),
    )
    half_pieces = lax.dynamic_slice(
        pieces, (1, 0, depth_index * lat_size + lat_index, 0, 0), (1, 2, 1, rows * SUBLANES, LANES)
    )
    stay = jnp.concatenate(
        [part.reshape(-1, LANES) for part in (own_pieces, half_pieces)]
        + [chunks[0][height - 3 * rows:]], axis=0,
    )
    middle = lat_size // 2
    order = sorted(range(1, lat_size), key=lambda turn: abs(turn - middle))
    waves = [stay] + [None] * (lat_size - 1)
    for turn in order:
        around = [(source, (source + turn) % lat_size) for source in range(lat_size)]
        waves[turn] = lax.ppermute(chunks[turn - 1], "lat", around)

    spread = pl.pallas_call(
        functools.partial(level_kernel, lat_size, freq_size, slots, levels),
        out_shape=jax.ShapeDtypeStruct((levels, lat_size, freq_size, rows, LANES), jnp.float32),
        in_specs=[SMEM_SPACE] * 2 + [VMEM_SPACE] * (lat_size + 3),
        out_specs=VMEM_SPACE,
        scratch_shapes=[
            pltpu.VMEM(((blocks * entries + 1) * 2 * (own + half), LANES), jnp.float32),
            pltpu.VMEM((entries * own, 2 * TILE), jnp.bfloat16),
            pltpu.VMEM((entries * half, 2 * TILE), jnp.bfloat16),
            pltpu.VMEM((levels * entries, SUBLANES, LANES), jnp.float32),
            pltpu.VMEM((entries, LANES), jnp.float32),
            pltpu.VMEM((levels, entries, LANES), jnp.float32),
            pltpu.VMEM((levels, entries, LANES), jnp.int32),
            pltpu.SMEM((levels, entries, LANES), jnp.int32),
            pltpu.SemaphoreType.DMA,
        ],
        cost_estimate=pl.CostEstimate(
            flops=8 * levels * blocks * entries * (own + half) * TILE * TILE,
            bytes_accessed=4 * entries * (own + half) * TILE + 16 * blocks * TILE * TILE,
            transcendentals=0,
        ),
        compiler_params=pltpu.CompilerParams(vmem_limit_bytes=32 << 20),
        name="levels",
    )(depth_id, lat_id, *waves, pool, remote_own, remote_half)
    spread = spread.reshape(levels * lat_size * freq_size, rows, LANES)
    parts = lax.all_to_all(spread, ("depth", "lat", "freq"), 0, 0, tiled=True)
    summed = jnp.sum(parts, axis=0).reshape(1, lateral_width)
    kept = 1.0 - refl
    factor = jnp.where(depth_index == levels - 1, kept * kept, 1.0)
    return summed * factor / (freqs_here * freq_size * shot_total)


def fits_fast(mesh, surface, pool, tile_ids):
    depth, lat, freq = (mesh.shape[name] for name in ("depth", "lat", "freq"))
    freqs, _, shots, width = surface.shape
    rows, slots = tile_ids.shape[1:]
    return (
        depth == 2
        and pool.shape[0] == depth
        and freqs == 3 * freq
        and shots == PACKED * lat
        and TILE == LANES
        and rows * TILE == width
        and rows == SUBLANES * lat
        and 2 * slots < HALF
        and max(rows, pool.shape[2]) <= 256
    )


def solution(mesh):
    placed = (
        P("freq", None, None, "lat"),
        P("depth", "lat"),
        P("depth", "freq", None, None, None),
        P("depth", "lat", None),
        P("depth", "lat", None),
        P("depth", "lat"),
    )

    def whole(surface, refl, pool, tile_ids, block_ids, counts):
        fast = fits_fast(mesh, surface, pool, tile_ids)
        mapped = jax.shard_map(
            per_device_fast if fast else per_device, mesh=mesh, in_specs=placed,
            out_specs=P("depth", "lat"), check_vma=False,
        )
        return mapped(surface, refl, pool, tile_ids, block_ids, counts)

    return whole
```

```python
import functools

import jax
import jax.numpy as jnp
from jax import lax
from jax.experimental import pallas as pl
from jax.experimental.pallas import tpu as pltpu
from jax.sharding import PartitionSpec as P


TILE = 128
TILE_DEV = 8


def extended_2(block, sides, width):
    for axis, dim in sides:
        count = lax.axis_size(axis)
        forward = [(i, i + 1) for i in range(count - 1)]
        forward.append((count - 1, 0))
        backward = [(target, source) for source, target in forward]
        low = lax.ppermute(
            lax.slice_in_dim(block, block.shape[dim] - width, None, axis=dim), axis, forward
        )
        high = lax.ppermute(lax.slice_in_dim(block, 0, width, axis=dim), axis, backward)
        block = jnp.concatenate([low, block, high], axis=dim)
    return block


def aperture_rim(wave_field):
    return extended_2(wave_field, (("lat", 3),), TILE_DEV * TILE)


def extrapolate(extended, pool_level, local_ids, block_level, count_level, refl_level):
    freqs_here = extended.shape[0]
    shot_rows = extended.shape[2]
    tile_rows = local_ids.shape[0]
    slot_total = local_ids.shape[1]
    tile_grid = extended.reshape(freqs_here, 2, shot_rows, -1, TILE)
    slot_live = (jnp.arange(slot_total)[None, :] < count_level[:, None]).astype(jnp.bfloat16)
    picked = jnp.take(tile_grid, local_ids, axis=3) * slot_live[None, None, None, :, :, None]
    chosen = jnp.take(pool_level, block_level, axis=1)
    product = jnp.einsum("fsarkt,frktc->rfsac", picked, chosen, preferred_element_type=jnp.float32)
    real_part = product[:, :, 0, :, :TILE] - product[:, :, 1, :, TILE:]
    imag_part = product[:, :, 0, :, TILE:] + product[:, :, 1, :, :TILE]
    row_scale = 1.0 / jnp.sqrt(count_level.astype(jnp.float32))
    rows_out = jnp.stack([real_part, imag_part], 2) * row_scale[:, None, None, None, None]
    wave_out = jnp.transpose(rows_out, (1, 2, 3, 0, 4)).reshape(
        freqs_here, 2, shot_rows, tile_rows * TILE
    )
    wave_out = wave_out * (1.0 - refl_level)
    return (wave_out.astype(jnp.bfloat16), jnp.sum(wave_out * wave_out, axis=(0, 1, 2)))


def per_device(surface, refl, pool, tile_ids, block_ids, counts):
    depth_index = lax.axis_index("depth")
    lat_index = lax.axis_index("lat")
    tile_count = TILE_DEV * lax.axis_size("lat")
    first_tile = lat_index * TILE_DEV - TILE_DEV
    freqs_here = surface.shape[0]
    shot_total = surface.shape[2]
    lateral_width = surface.shape[3]
    shot_rows = shot_total // lax.axis_size("depth")
    own_shots = lax.dynamic_slice_in_dim(surface, depth_index * shot_rows, shot_rows, 2)
    pool_all = lax.all_gather(pool, "depth", axis=0, tiled=True)
    ids_all, blocks_all, counts_all = (
        lax.all_gather(tile_ids, "depth", axis=0, tiled=True),
        lax.all_gather(block_ids, "depth", axis=0, tiled=True),
        lax.all_gather(counts, "depth", axis=0, tiled=True),
    )
    refl_all = lax.all_gather(refl, "depth", axis=0, tiled=True)
    level_total = pool_all.shape[0]

    def level_step(level_index, loop_state):
        wave_field, images = loop_state
        ids_here = lax.dynamic_index_in_dim(ids_all, level_index, 0, keepdims=False)
        local_level = jnp.mod(ids_here - first_tile, tile_count)
        pool_here = lax.dynamic_index_in_dim(pool_all, level_index, 0, keepdims=False)
        blocks_here = lax.dynamic_index_in_dim(blocks_all, level_index, 0, keepdims=False)
        counts_here = lax.dynamic_index_in_dim(counts_all, level_index, 0, keepdims=False)
        refl_here = lax.dynamic_index_in_dim(refl_all, level_index, 0, keepdims=False)
        handed, partial_value = extrapolate(
            aperture_rim(wave_field), pool_here, local_level, blocks_here, counts_here, refl_here
        )
        images = lax.dynamic_update_index_in_dim(images, partial_value, level_index, 0)
        return (handed, images)

    start_images = jnp.zeros((level_total, lateral_width), jnp.float32)
    loop_state = lax.fori_loop(0, level_total, level_step, (own_shots, start_images))
    image_local = lax.psum_scatter(loop_state[1], "depth", scatter_dimension=0, tiled=True)[0]
    summed = lax.psum(image_local, "freq")
    divisor = freqs_here * lax.axis_size("freq") * shot_total
    return (summed / divisor)[None, :]


ROWS_STEP = 4
FAR = 1
LANES = 128
SUBLANES = 8
HALF = LANES // 2
PACKED = 16
VMEM_SPACE = pl.BlockSpec(memory_space=pltpu.VMEM)
SMEM_SPACE = pl.BlockSpec(memory_space=pltpu.SMEM)
ANY_SPACE = pl.BlockSpec(memory_space=pl.ANY)


def chunk_copies(surface_ref, depth_index, target, lat_size, out, sems):
    groups = surface_ref.shape[2] // lat_size
    height = surface_ref.shape[3]
    sources = [
        surface_ref.at[2 * depth_index, part, groups * target + group]
        for part in range(2)
        for group in range(groups)
    ] + [surface_ref.at[1, part, depth_index * lat_size + target] for part in range(2)]
    return [
        pltpu.make_async_copy(source, out.at[pl.ds(place * height, height), :], sems.at[place])
        for place, source in enumerate(sources)
    ]


def first_kernel(
    lat_size, turns, depth_ref, lat_ref, surface_ref, pool_ref, refl_ref, tiles_ref, blocks_ref,
    counts_ref, *refs,
):
    out_ref, own_ref, half_ref = refs[:3]
    chunks, sems = refs[3:-1], refs[-1]
    depth_index = depth_ref[0]
    copies = [
        pltpu.make_async_copy(pool_ref.at[0, 2 * (1 - depth_index)], own_ref, sems.at[len(turns), 0]),
        pltpu.make_async_copy(pool_ref.at[0, 1], half_ref, sems.at[len(turns), 1]),
    ]
    for place, turn in enumerate(turns):
        target = lax.rem(lat_ref[0] + turn, lat_size)
        copies += chunk_copies(
            surface_ref, depth_index, target, lat_size, chunks[place], sems.at[place]
        )
    for copy in copies:
        copy.start()
    rows = tiles_ref.shape[1]
    slots = tiles_ref.shape[2]
    for row in range(rows):
        out_ref[row:row + 1, :] = refl_ref[:, row * LANES:(row + 1) * LANES]
    out_ref[rows:, :] = jnp.zeros((rows, LANES), jnp.float32)
    out_ref[rows:, :slots] = blocks_ref[0].astype(jnp.float32)
    out_ref[rows:, slots:2 * slots] = tiles_ref[0].astype(jnp.float32)
    spread = jnp.broadcast_to(counts_ref[...].astype(jnp.float32), (rows, rows))
    across = lax.broadcasted_iota(jnp.int32, (rows, rows), 1)
    down = lax.broadcasted_iota(jnp.int32, (rows, rows), 0)
    column = jnp.sum(jnp.where(across == down, spread, 0.0), axis=1, keepdims=True)
    out_ref[rows:, 2 * slots:2 * slots + 1] = column
    for copy in copies:
        copy.wait()


def second_kernel(lat_size, turns, depth_ref, lat_ref, surface_ref, mine_ref, other_ref, *refs):
    chunks, lists_ref, sems = refs[:-2], refs[-2], refs[-1]
    depth_index = depth_ref[0]
    rows = mine_ref.shape[0] // 2
    copies = []
    for place, turn in enumerate(turns):
        target = lax.rem(lat_ref[0] + turn, lat_size)
        copies += chunk_copies(
            surface_ref, depth_index, target, lat_size, chunks[place], sems.at[place]
        )
    for copy in copies:
        copy.start()
    first = jnp.where(depth_index == 0, mine_ref[...], other_ref[...])
    second = jnp.where(depth_index == 0, other_ref[rows:, :], mine_ref[rows:, :])
    refl = first[:rows]
    high = refl.astype(jnp.bfloat16).astype(jnp.float32)
    pair = jnp.concatenate([high, refl - high], axis=0).astype(jnp.bfloat16)
    lists = (first[rows:] + pltpu.roll(second, HALF, 1)).astype(jnp.bfloat16)
    for out in [*chunks, lists_ref]:
        start = out.shape[0] - 3 * rows
        out[start:start + 2 * rows, :] = pair
        out[start + 2 * rows:, :] = lists
    for copy in copies:
        copy.wait()


def level_kernel(lat_size, freq_size, slots, levels, depth_ref, lat_ref, *refs):
    wave_refs, tail_refs, refs = refs[:lat_size], refs[lat_size:2 * lat_size], refs[2 * lat_size:]
    (local_ref, remote_own_ref, remote_half_ref, image_ref, table, own_buf, half_buf, squares_buf,
     lists_buf, factor_buf, index_buf, index_ref, sem) = refs
    blocks = remote_own_ref.shape[0]
    entries = factor_buf.shape[1]
    rows = entries // lat_size
    own = own_buf.shape[0] // entries
    half = own // 2
    unit = 2 * (own + half)
    depth_index = depth_ref[0]
    for turn, tail in enumerate(tail_refs):
        source = lax.rem(lat_ref[0] + lat_size - turn, lat_size)
        top = tail.shape[0] - 3 * rows
        pair = tail[top:top + 2 * rows, :].astype(jnp.float32)
        high, low = pair[:rows], pair[rows:]
        lists = tail[top + 2 * rows:, :].astype(jnp.float32)
        start = pl.multiple_of(source * rows, rows)
        factor_buf[0, pl.ds(start, rows), :] = 1.0 - (high + low)
        lists_buf[pl.ds(start, rows), :] = lists
    lane = lax.broadcasted_iota(jnp.int32, (entries, LANES), 1).astype(jnp.float32)
    for level in range(levels):
        listed = lists_buf[...]
        if level:
            listed = pltpu.roll(listed, LANES - HALF, 1)
        count = jnp.broadcast_to(listed[:, 2 * slots:2 * slots + 1], (entries, LANES))
        tile = pltpu.roll(listed, LANES - slots, 1)
        place = jnp.where(lane < count, listed * entries + tile, float(blocks * entries))
        index_buf[level] = (place * unit).astype(jnp.int32)
        scale = 1.0 / jnp.sqrt(count)
        factor_buf[level] = scale if level == levels - 1 else scale * factor_buf[level]
    index_copy = pltpu.make_async_copy(index_buf, index_ref, sem)
    index_copy.start()
    table[blocks * entries * unit:, :] = jnp.zeros((unit, LANES), jnp.float32)

    for turn, wave in enumerate(wave_refs):
        source = lax.rem(lat_ref[0] + lat_size - turn, lat_size)

        height = rows * SUBLANES
        for part in range(2):
            lanes = slice(part * LANES, (part + 1) * LANES)
            for group in range(2):
                start = pl.multiple_of((source * 2 + group) * height, height)
                place = (part * 2 + group) * height
                own_buf[pl.ds(start, height), lanes] = wave[place:place + height, :]
            start = pl.multiple_of(source * height, height)
            place = (4 + part) * height
            half_buf[pl.ds(start, height), lanes] = wave[place:place + height, :]

    def weights_of(level, local, remote):
        upper = jnp.where(depth_index == level, local, remote)
        lower = jnp.concatenate([-upper[:, TILE:], upper[:, :TILE]], axis=1)
        return jnp.concatenate([upper, lower], axis=0)

    def units(product, groups):
        sources = lat_size if groups else 1
        product = product.reshape(sources, max(groups, 1), entries // sources, -1, 2 * TILE)
        return [
            product[:, group, :, :, part * TILE:(part + 1) * TILE].reshape(entries, -1, TILE)
            for part in range(2)
            for group in range(max(groups, 1))
        ]

    for level in range(levels):
        last = level == levels - 1

        def block_step(block, carry):
            weights_own = weights_of(
                level, local_ref[0, 2 * depth_index, block], remote_own_ref[block]
            )
            weights_half = weights_of(level, local_ref[0, 1, block], remote_half_ref[block])
            product_own = jnp.dot(own_buf[...], weights_own, preferred_element_type=jnp.float32)
            product_half = jnp.dot(half_buf[...], weights_half, preferred_element_type=jnp.float32)
            joined = units(product_own, 0 if level else own // SUBLANES) + units(product_half, 0)
            start = pl.multiple_of(block * entries * unit, entries * unit)
            table[pl.ds(start, entries * unit), :] = jnp.concatenate(joined, axis=1).reshape(
                entries * unit, LANES
            )
            return carry

        lax.fori_loop(0, blocks, block_step, 0, unroll=4)
        if level == 0:
            index_copy.wait()

        def row_step(step, carry):
            outs = []
            for inner in range(ROWS_STEP):
                row = step * ROWS_STEP + inner
                total = None
                for slot in range(slots):
                    start = pl.multiple_of(index_ref[level, row, slot], SUBLANES)
                    term = table[pl.ds(start, unit), :]
                    total = term if total is None else total + term
                total = total * factor_buf[level, pl.ds(row, 1), :]
                outs.append(total)
                squares = total * total
                squares_buf[level * entries + row] = jnp.sum(
                    squares.reshape(unit // SUBLANES, SUBLANES, LANES), axis=0
                )
            if not last:
                for k, out in enumerate(outs):
                    start = pl.multiple_of((step * ROWS_STEP + k) * own, own)
                    own_buf[pl.ds(start, own), :] = jnp.concatenate(
                        [out[:own], out[own:2 * own]], axis=1
                    ).astype(jnp.bfloat16)
                for k in range(0, ROWS_STEP, 2):
                    pair = outs[k:k + 2]
                    real = jnp.concatenate([out[2 * own:2 * own + half] for out in pair], axis=0)
                    imag = jnp.concatenate([out[2 * own + half:] for out in pair], axis=0)
                    start = pl.multiple_of((step * ROWS_STEP + k) * half, 2 * half)
                    half_buf[pl.ds(start, 2 * half), :] = jnp.concatenate(
                        [real, imag], axis=1
                    ).astype(jnp.bfloat16)
            return carry

        lax.fori_loop(0, entries // ROWS_STEP, row_step, 0)

    summed = jnp.sum(squares_buf[...], axis=1)
    for level in range(levels):
        for target in range(lat_size):
            start = level * entries + target * rows
            for copy in range(freq_size):
                image_ref[level, target, copy] = summed[start:start + rows]


def turns_of(lat_size):
    turns = sorted(range(1, lat_size), key=lambda turn: abs(turn - lat_size // 2))
    return turns[:FAR], turns[FAR:]


def per_device_fast(surface, refl, pool, tile_ids, block_ids, counts):
    depth_index = lax.axis_index("depth")
    lat_index = lax.axis_index("lat")
    levels = lax.axis_size("depth")
    lat_size = lax.axis_size("lat")
    freq_size = lax.axis_size("freq")
    freqs_here, _, shot_total, lateral_width = surface.shape
    rows, slots = tile_ids.shape[1:]
    blocks = pool.shape[2]
    entries = rows * lat_size
    own = shot_total // lat_size
    half = own // 2
    swap = [(0, 1), (1, 0)]
    depth_id = depth_index.astype(jnp.int32).reshape(1)
    lat_id = lat_index.astype(jnp.int32).reshape(1)

    pieces = surface.reshape(
        freqs_here, 2, shot_total // SUBLANES, SUBLANES, rows, LANES
    ).transpose(0, 1, 2, 4, 3, 5).reshape(
        freqs_here, 2, shot_total // SUBLANES, rows * SUBLANES, LANES
    )
    cuts = 2 * (own + half) // SUBLANES
    height = cuts * rows * SUBLANES
    tail = 3 * rows
    far, near = turns_of(lat_size)

    def bf16_out(length):
        return jax.ShapeDtypeStruct((length, LANES), jnp.bfloat16)

    sent = jax.ShapeDtypeStruct(pool.shape[2:], pool.dtype)
    mine, send_own, send_half, *far_chunks = pl.pallas_call(
        functools.partial(first_kernel, lat_size, far),
        out_shape=[jax.ShapeDtypeStruct((2 * rows, LANES), jnp.float32), sent, sent]
        + [bf16_out(height)] * len(far),
        in_specs=[SMEM_SPACE] * 2 + [ANY_SPACE] * 2 + [VMEM_SPACE] * 4,
        out_specs=[VMEM_SPACE] * (3 + len(far)),
        scratch_shapes=[pltpu.SemaphoreType.DMA((len(far) + 1, cuts))],
        name="first",
    )(depth_id, lat_id, pieces, pool, refl, tile_ids, block_ids, counts)
    other = lax.ppermute(mine, "depth", swap)
    remote_own = lax.ppermute(send_own, "depth", swap)
    remote_half = lax.ppermute(send_half, "depth", swap)
    waves, tails = {}, {}

    def around(turn):
        return [(source, (source + turn) % lat_size) for source in range(lat_size)]

    for turn, chunk in zip(far, far_chunks):
        waves[turn] = lax.ppermute(chunk, "lat", around(turn))
    *near_chunks, stay, lists = pl.pallas_call(
        functools.partial(second_kernel, lat_size, near + [0]),
        out_shape=[bf16_out(height + tail)] * (len(near) + 1) + [bf16_out(tail)],
        in_specs=[SMEM_SPACE] * 2 + [ANY_SPACE] + [VMEM_SPACE] * 2,
        out_specs=[VMEM_SPACE] * (len(near) + 2),
        scratch_shapes=[pltpu.SemaphoreType.DMA((len(near) + 1, cuts))],
        compiler_params=pltpu.CompilerParams(vmem_limit_bytes=8 << 20),
        name="second",
    )(depth_id, lat_id, pieces, mine, other)
    for turn, chunk in zip(near, near_chunks):
        tails[turn] = waves[turn] = lax.ppermute(chunk, "lat", around(turn))
    for turn in far:
        tails[turn] = lax.ppermute(lists, "lat", around(turn))
    waves[0] = tails[0] = stay
    waves = [waves[turn] for turn in range(lat_size)]
    tails = [tails[turn] for turn in range(lat_size)]

    spread = pl.pallas_call(
        functools.partial(level_kernel, lat_size, freq_size, slots, levels),
        out_shape=jax.ShapeDtypeStruct((levels, lat_size, freq_size, rows, LANES), jnp.float32),
        in_specs=[SMEM_SPACE] * 2 + [VMEM_SPACE] * (2 * lat_size + 3),
        out_specs=VMEM_SPACE,
        scratch_shapes=[
            pltpu.VMEM(((blocks * entries + 1) * 2 * (own + half), LANES), jnp.float32),
            pltpu.VMEM((entries * own, 2 * TILE), jnp.bfloat16),
            pltpu.VMEM((entries * half, 2 * TILE), jnp.bfloat16),
            pltpu.VMEM((levels * entries, SUBLANES, LANES), jnp.float32),
            pltpu.VMEM((entries, LANES), jnp.float32),
            pltpu.VMEM((levels, entries, LANES), jnp.float32),
            pltpu.VMEM((levels, entries, LANES), jnp.int32),
            pltpu.SMEM((levels, entries, LANES), jnp.int32),
            pltpu.SemaphoreType.DMA,
        ],
        cost_estimate=pl.CostEstimate(
            flops=8 * levels * blocks * entries * (own + half) * TILE * TILE,
            bytes_accessed=4 * entries * (own + half) * TILE + 16 * blocks * TILE * TILE,
            transcendentals=0,
        ),
        compiler_params=pltpu.CompilerParams(vmem_limit_bytes=32 << 20),
        name="levels",
    )(depth_id, lat_id, *waves, *tails, pool, remote_own, remote_half)
    spread = spread.reshape(levels * lat_size * freq_size, rows, LANES)
    parts = lax.all_to_all(spread, ("depth", "lat", "freq"), 0, 0, tiled=True)
    summed = jnp.sum(parts, axis=0).reshape(1, lateral_width)
    kept = 1.0 - refl
    factor = jnp.where(depth_index == levels - 1, kept * kept, 1.0)
    return summed * factor / (freqs_here * freq_size * shot_total)


def fits_fast(mesh, surface, pool, tile_ids):
    depth, lat, freq = (mesh.shape[name] for name in ("depth", "lat", "freq"))
    freqs, _, shots, width = surface.shape
    rows, slots = tile_ids.shape[1:]
    return (
        depth == 2
        and pool.shape[0] == depth
        and freqs == 3 * freq
        and shots == PACKED * lat
        and TILE == LANES
        and rows * TILE == width
        and rows == SUBLANES * lat
        and 2 * slots < HALF
        and max(rows, pool.shape[2]) <= 256
    )


def solution(mesh):
    placed = (
        P("freq", None, None, "lat"),
        P("depth", "lat"),
        P("depth", "freq", None, None, None),
        P("depth", "lat", None),
        P("depth", "lat", None),
        P("depth", "lat"),
    )

    def whole(surface, refl, pool, tile_ids, block_ids, counts):
        fast = fits_fast(mesh, surface, pool, tile_ids)
        mapped = jax.shard_map(
            per_device_fast if fast else per_device, mesh=mesh, in_specs=placed,
            out_specs=P("depth", "lat"), check_vma=False,
        )
        return mapped(surface, refl, pool, tile_ids, block_ids, counts)

    return whole
```

```python
import functools

import jax
import jax.numpy as jnp
from jax import lax
from jax.experimental import pallas as pl
from jax.experimental.pallas import tpu as pltpu
from jax.sharding import PartitionSpec as P


TILE = 128
TILE_DEV = 8


def extended_2(block, sides, width):
    for axis, dim in sides:
        count = lax.axis_size(axis)
        forward = [(i, i + 1) for i in range(count - 1)]
        forward.append((count - 1, 0))
        backward = [(target, source) for source, target in forward]
        low = lax.ppermute(
            lax.slice_in_dim(block, block.shape[dim] - width, None, axis=dim), axis, forward
        )
        high = lax.ppermute(lax.slice_in_dim(block, 0, width, axis=dim), axis, backward)
        block = jnp.concatenate([low, block, high], axis=dim)
    return block


def aperture_rim(wave_field):
    return extended_2(wave_field, (("lat", 3),), TILE_DEV * TILE)


def extrapolate(extended, pool_level, local_ids, block_level, count_level, refl_level):
    freqs_here = extended.shape[0]
    shot_rows = extended.shape[2]
    tile_rows = local_ids.shape[0]
    slot_total = local_ids.shape[1]
    tile_grid = extended.reshape(freqs_here, 2, shot_rows, -1, TILE)
    slot_live = (jnp.arange(slot_total)[None, :] < count_level[:, None]).astype(jnp.bfloat16)
    picked = jnp.take(tile_grid, local_ids, axis=3) * slot_live[None, None, None, :, :, None]
    chosen = jnp.take(pool_level, block_level, axis=1)
    product = jnp.einsum("fsarkt,frktc->rfsac", picked, chosen, preferred_element_type=jnp.float32)
    real_part = product[:, :, 0, :, :TILE] - product[:, :, 1, :, TILE:]
    imag_part = product[:, :, 0, :, TILE:] + product[:, :, 1, :, :TILE]
    row_scale = 1.0 / jnp.sqrt(count_level.astype(jnp.float32))
    rows_out = jnp.stack([real_part, imag_part], 2) * row_scale[:, None, None, None, None]
    wave_out = jnp.transpose(rows_out, (1, 2, 3, 0, 4)).reshape(
        freqs_here, 2, shot_rows, tile_rows * TILE
    )
    wave_out = wave_out * (1.0 - refl_level)
    return (wave_out.astype(jnp.bfloat16), jnp.sum(wave_out * wave_out, axis=(0, 1, 2)))


def per_device(surface, refl, pool, tile_ids, block_ids, counts):
    depth_index = lax.axis_index("depth")
    lat_index = lax.axis_index("lat")
    tile_count = TILE_DEV * lax.axis_size("lat")
    first_tile = lat_index * TILE_DEV - TILE_DEV
    freqs_here = surface.shape[0]
    shot_total = surface.shape[2]
    lateral_width = surface.shape[3]
    shot_rows = shot_total // lax.axis_size("depth")
    own_shots = lax.dynamic_slice_in_dim(surface, depth_index * shot_rows, shot_rows, 2)
    pool_all = lax.all_gather(pool, "depth", axis=0, tiled=True)
    ids_all, blocks_all, counts_all = (
        lax.all_gather(tile_ids, "depth", axis=0, tiled=True),
        lax.all_gather(block_ids, "depth", axis=0, tiled=True),
        lax.all_gather(counts, "depth", axis=0, tiled=True),
    )
    refl_all = lax.all_gather(refl, "depth", axis=0, tiled=True)
    level_total = pool_all.shape[0]

    def level_step(level_index, loop_state):
        wave_field, images = loop_state
        ids_here = lax.dynamic_index_in_dim(ids_all, level_index, 0, keepdims=False)
        local_level = jnp.mod(ids_here - first_tile, tile_count)
        pool_here = lax.dynamic_index_in_dim(pool_all, level_index, 0, keepdims=False)
        blocks_here = lax.dynamic_index_in_dim(blocks_all, level_index, 0, keepdims=False)
        counts_here = lax.dynamic_index_in_dim(counts_all, level_index, 0, keepdims=False)
        refl_here = lax.dynamic_index_in_dim(refl_all, level_index, 0, keepdims=False)
        handed, partial_value = extrapolate(
            aperture_rim(wave_field), pool_here, local_level, blocks_here, counts_here, refl_here
        )
        images = lax.dynamic_update_index_in_dim(images, partial_value, level_index, 0)
        return (handed, images)

    start_images = jnp.zeros((level_total, lateral_width), jnp.float32)
    loop_state = lax.fori_loop(0, level_total, level_step, (own_shots, start_images))
    image_local = lax.psum_scatter(loop_state[1], "depth", scatter_dimension=0, tiled=True)[0]
    summed = lax.psum(image_local, "freq")
    divisor = freqs_here * lax.axis_size("freq") * shot_total
    return (summed / divisor)[None, :]


ROWS_STEP = 4
FAR = 2
LANES = 128
SUBLANES = 8
HALF = LANES // 2
PACKED = 16
VMEM_SPACE = pl.BlockSpec(memory_space=pltpu.VMEM)
SMEM_SPACE = pl.BlockSpec(memory_space=pltpu.SMEM)
ANY_SPACE = pl.BlockSpec(memory_space=pl.ANY)


def chunk_copies(surface_ref, depth_index, target, lat_size, out, sems):
    groups = surface_ref.shape[2] // lat_size
    height = surface_ref.shape[3]
    sources = [
        surface_ref.at[2 * depth_index, part, groups * target + group]
        for part in range(2)
        for group in range(groups)
    ] + [surface_ref.at[1, part, depth_index * lat_size + target] for part in range(2)]
    return [
        pltpu.make_async_copy(source, out.at[pl.ds(place * height, height), :], sems.at[place])
        for place, source in enumerate(sources)
    ]


def first_kernel(
    lat_size, turns, depth_ref, lat_ref, surface_ref, pool_ref, refl_ref, tiles_ref, blocks_ref,
    counts_ref, *refs,
):
    out_ref, own_ref, half_ref = refs[:3]
    chunks, sems = refs[3:-1], refs[-1]
    depth_index = depth_ref[0]
    copies = [
        pltpu.make_async_copy(pool_ref.at[0, 2 * (1 - depth_index)], own_ref, sems.at[len(turns), 0]),
        pltpu.make_async_copy(pool_ref.at[0, 1], half_ref, sems.at[len(turns), 1]),
    ]
    for place, turn in enumerate(turns):
        target = lax.rem(lat_ref[0] + turn, lat_size)
        copies += chunk_copies(
            surface_ref, depth_index, target, lat_size, chunks[place], sems.at[place]
        )
    for copy in copies:
        copy.start()
    rows = tiles_ref.shape[1]
    slots = tiles_ref.shape[2]
    for row in range(rows):
        out_ref[row:row + 1, :] = refl_ref[:, row * LANES:(row + 1) * LANES]
    out_ref[rows:, :] = jnp.zeros((rows, LANES), jnp.float32)
    out_ref[rows:, :slots] = blocks_ref[0].astype(jnp.float32)
    out_ref[rows:, slots:2 * slots] = tiles_ref[0].astype(jnp.float32)
    spread = jnp.broadcast_to(counts_ref[...].astype(jnp.float32), (rows, rows))
    across = lax.broadcasted_iota(jnp.int32, (rows, rows), 1)
    down = lax.broadcasted_iota(jnp.int32, (rows, rows), 0)
    column = jnp.sum(jnp.where(across == down, spread, 0.0), axis=1, keepdims=True)
    out_ref[rows:, 2 * slots:2 * slots + 1] = column
    for copy in copies:
        copy.wait()


def second_kernel(lat_size, turns, depth_ref, lat_ref, surface_ref, mine_ref, other_ref, *refs):
    chunks, lists_ref, sems = refs[:-2], refs[-2], refs[-1]
    depth_index = depth_ref[0]
    rows = mine_ref.shape[0] // 2
    copies = []
    for place, turn in enumerate(turns):
        target = lax.rem(lat_ref[0] + turn, lat_size)
        copies += chunk_copies(
            surface_ref, depth_index, target, lat_size, chunks[place], sems.at[place]
        )
    for copy in copies:
        copy.start()
    first = jnp.where(depth_index == 0, mine_ref[...], other_ref[...])
    second = jnp.where(depth_index == 0, other_ref[rows:, :], mine_ref[rows:, :])
    refl = first[:rows]
    high = refl.astype(jnp.bfloat16).astype(jnp.float32)
    pair = jnp.concatenate([high, refl - high], axis=0).astype(jnp.bfloat16)
    lists = (first[rows:] + pltpu.roll(second, HALF, 1)).astype(jnp.bfloat16)
    for out in [*chunks, lists_ref]:
        start = out.shape[0] - 3 * rows
        out[start:start + 2 * rows, :] = pair
        out[start + 2 * rows:, :] = lists
    for copy in copies:
        copy.wait()


def level_kernel(lat_size, freq_size, slots, levels, depth_ref, lat_ref, *refs):
    wave_refs, tail_refs, refs = refs[:lat_size], refs[lat_size:2 * lat_size], refs[2 * lat_size:]
    (local_ref, remote_own_ref, remote_half_ref, image_ref, table, own_buf, half_buf, squares_buf,
     lists_buf, factor_buf, index_buf, index_ref, sem) = refs
    blocks = remote_own_ref.shape[0]
    entries = factor_buf.shape[1]
    rows = entries // lat_size
    own = own_buf.shape[0] // entries
    half = own // 2
    unit = 2 * (own + half)
    depth_index = depth_ref[0]
    for turn, tail in enumerate(tail_refs):
        source = lax.rem(lat_ref[0] + lat_size - turn, lat_size)
        top = tail.shape[0] - 3 * rows
        pair = tail[top:top + 2 * rows, :].astype(jnp.float32)
        high, low = pair[:rows], pair[rows:]
        lists = tail[top + 2 * rows:, :].astype(jnp.float32)
        start = pl.multiple_of(source * rows, rows)
        factor_buf[0, pl.ds(start, rows), :] = 1.0 - (high + low)
        lists_buf[pl.ds(start, rows), :] = lists
    lane = lax.broadcasted_iota(jnp.int32, (entries, LANES), 1).astype(jnp.float32)
    for level in range(levels):
        listed = lists_buf[...]
        if level:
            listed = pltpu.roll(listed, LANES - HALF, 1)
        count = jnp.broadcast_to(listed[:, 2 * slots:2 * slots + 1], (entries, LANES))
        tile = pltpu.roll(listed, LANES - slots, 1)
        place = jnp.where(lane < count, listed * entries + tile, float(blocks * entries))
        place = place * unit
        if level:
            placed = jnp.where(lane < HALF, placed, pltpu.roll(place, level * HALF, 1))
        else:
            placed = place
        scale = 1.0 / jnp.sqrt(count)
        factor_buf[level] = scale if level == levels - 1 else scale * factor_buf[level]
    index_buf[...] = placed.astype(jnp.int32)
    index_copy = pltpu.make_async_copy(index_buf, index_ref, sem)
    index_copy.start()
    table[blocks * entries * unit:, :] = jnp.zeros((unit, LANES), jnp.float32)

    for turn, wave in enumerate(wave_refs):
        source = lax.rem(lat_ref[0] + lat_size - turn, lat_size)

        height = rows * SUBLANES
        for part in range(2):
            lanes = slice(part * LANES, (part + 1) * LANES)
            for group in range(2):
                start = pl.multiple_of((source * 2 + group) * height, height)
                place = (part * 2 + group) * height
                own_buf[pl.ds(start, height), lanes] = wave[place:place + height, :]
            start = pl.multiple_of(source * height, height)
            place = (4 + part) * height
            half_buf[pl.ds(start, height), lanes] = wave[place:place + height, :]

    def weights_of(level, local, remote):
        upper = jnp.where(depth_index == level, local, remote)
        lower = jnp.concatenate([-upper[:, TILE:], upper[:, :TILE]], axis=1)
        return jnp.concatenate([upper, lower], axis=0)

    def units(product, groups):
        sources = lat_size if groups else 1
        product = product.reshape(sources, max(groups, 1), entries // sources, -1, 2 * TILE)
        return [
            product[:, group, :, :, part * TILE:(part + 1) * TILE].reshape(entries, -1, TILE)
            for part in range(2)
            for group in range(max(groups, 1))
        ]

    for level in range(levels):
        last = level == levels - 1

        def block_step(block, carry):
            weights_own = weights_of(
                level, local_ref[0, 2 * depth_index, block], remote_own_ref[block]
            )
            weights_half = weights_of(level, local_ref[0, 1, block], remote_half_ref[block])
            product_own = jnp.dot(own_buf[...], weights_own, preferred_element_type=jnp.float32)
            product_half = jnp.dot(half_buf[...], weights_half, preferred_element_type=jnp.float32)
            joined = units(product_own, 0 if level else own // SUBLANES) + units(product_half, 0)
            start = pl.multiple_of(block * entries * unit, entries * unit)
            table[pl.ds(start, entries * unit), :] = jnp.concatenate(joined, axis=1).reshape(
                entries * unit, LANES
            )
            return carry

        lax.fori_loop(0, blocks, block_step, 0, unroll=4)
        if level == 0:
            index_copy.wait()

        def row_step(step, carry):
            outs = []
            for inner in range(ROWS_STEP):
                row = step * ROWS_STEP + inner
                total = None
                for slot in range(slots):
                    start = pl.multiple_of(index_ref[row, level * HALF + slot], SUBLANES)
                    term = table[pl.ds(start, unit), :]
                    total = term if total is None else total + term
                total = total * factor_buf[level, pl.ds(row, 1), :]
                outs.append(total)
                squares = total * total
                squares_buf[level * entries + row] = jnp.sum(
                    squares.reshape(unit // SUBLANES, SUBLANES, LANES), axis=0
                )
            if not last:
                for k, out in enumerate(outs):
                    start = pl.multiple_of((step * ROWS_STEP + k) * own, own)
                    own_buf[pl.ds(start, own), :] = jnp.concatenate(
                        [out[:own], out[own:2 * own]], axis=1
                    ).astype(jnp.bfloat16)
                for k in range(0, ROWS_STEP, 2):
                    pair = outs[k:k + 2]
                    real = jnp.concatenate([out[2 * own:2 * own + half] for out in pair], axis=0)
                    imag = jnp.concatenate([out[2 * own + half:] for out in pair], axis=0)
                    start = pl.multiple_of((step * ROWS_STEP + k) * half, 2 * half)
                    half_buf[pl.ds(start, 2 * half), :] = jnp.concatenate(
                        [real, imag], axis=1
                    ).astype(jnp.bfloat16)
            return carry

        lax.fori_loop(0, entries // ROWS_STEP, row_step, 0, unroll=2)

    summed = jnp.sum(squares_buf[...], axis=1)
    for level in range(levels):
        for target in range(lat_size):
            start = level * entries + target * rows
            for copy in range(freq_size):
                image_ref[level, target, copy] = summed[start:start + rows]


def turns_of(lat_size):
    turns = sorted(range(1, lat_size), key=lambda turn: (abs(turn - lat_size // 2), -turn))
    return turns[:FAR], turns[FAR:]


def per_device_fast(surface, refl, pool, tile_ids, block_ids, counts):
    depth_index = lax.axis_index("depth")
    lat_index = lax.axis_index("lat")
    levels = lax.axis_size("depth")
    lat_size = lax.axis_size("lat")
    freq_size = lax.axis_size("freq")
    freqs_here, _, shot_total, lateral_width = surface.shape
    rows, slots = tile_ids.shape[1:]
    blocks = pool.shape[2]
    entries = rows * lat_size
    own = shot_total // lat_size
    half = own // 2
    swap = [(0, 1), (1, 0)]
    depth_id = depth_index.astype(jnp.int32).reshape(1)
    lat_id = lat_index.astype(jnp.int32).reshape(1)

    pieces = surface.reshape(
        freqs_here, 2, shot_total // SUBLANES, SUBLANES, rows, LANES
    ).transpose(0, 1, 2, 4, 3, 5).reshape(
        freqs_here, 2, shot_total // SUBLANES, rows * SUBLANES, LANES
    )
    cuts = 2 * (own + half) // SUBLANES
    height = cuts * rows * SUBLANES
    tail = 3 * rows
    far, near = turns_of(lat_size)

    def bf16_out(length):
        return jax.ShapeDtypeStruct((length, LANES), jnp.bfloat16)

    sent = jax.ShapeDtypeStruct(pool.shape[2:], pool.dtype)
    mine, send_own, send_half, *far_chunks = pl.pallas_call(
        functools.partial(first_kernel, lat_size, far),
        out_shape=[jax.ShapeDtypeStruct((2 * rows, LANES), jnp.float32), sent, sent]
        + [bf16_out(height)] * len(far),
        in_specs=[SMEM_SPACE] * 2 + [ANY_SPACE] * 2 + [VMEM_SPACE] * 4,
        out_specs=[VMEM_SPACE] * (3 + len(far)),
        scratch_shapes=[pltpu.SemaphoreType.DMA((len(far) + 1, cuts))],
        name="first",
    )(depth_id, lat_id, pieces, pool, refl, tile_ids, block_ids, counts)
    other = lax.ppermute(mine, "depth", swap)
    remote_own = lax.ppermute(send_own, "depth", swap)
    remote_half = lax.ppermute(send_half, "depth", swap)
    waves, tails = {}, {}

    def around(turn):
        return [(source, (source + turn) % lat_size) for source in range(lat_size)]

    for turn, chunk in zip(far, far_chunks):
        waves[turn] = lax.ppermute(chunk, "lat", around(turn))
    *near_chunks, stay, lists = pl.pallas_call(
        functools.partial(second_kernel, lat_size, near + [0]),
        out_shape=[bf16_out(height + tail)] * (len(near) + 1) + [bf16_out(tail)],
        in_specs=[SMEM_SPACE] * 2 + [ANY_SPACE] + [VMEM_SPACE] * 2,
        out_specs=[VMEM_SPACE] * (len(near) + 2),
        scratch_shapes=[pltpu.SemaphoreType.DMA((len(near) + 1, cuts))],
        compiler_params=pltpu.CompilerParams(vmem_limit_bytes=8 << 20),
        name="second",
    )(depth_id, lat_id, pieces, mine, other)
    for turn, chunk in zip(near, near_chunks):
        tails[turn] = waves[turn] = lax.ppermute(chunk, "lat", around(turn))
    for turn in far:
        tails[turn] = lax.ppermute(lists, "lat", around(turn))
    waves[0] = tails[0] = stay
    waves = [waves[turn] for turn in range(lat_size)]
    tails = [tails[turn] for turn in range(lat_size)]

    spread = pl.pallas_call(
        functools.partial(level_kernel, lat_size, freq_size, slots, levels),
        out_shape=jax.ShapeDtypeStruct((levels, lat_size, freq_size, rows, LANES), jnp.float32),
        in_specs=[SMEM_SPACE] * 2 + [VMEM_SPACE] * (2 * lat_size + 3),
        out_specs=VMEM_SPACE,
        scratch_shapes=[
            pltpu.VMEM(((blocks * entries + 1) * 2 * (own + half), LANES), jnp.float32),
            pltpu.VMEM((entries * own, 2 * TILE), jnp.bfloat16),
            pltpu.VMEM((entries * half, 2 * TILE), jnp.bfloat16),
            pltpu.VMEM((levels * entries, SUBLANES, LANES), jnp.float32),
            pltpu.VMEM((entries, LANES), jnp.float32),
            pltpu.VMEM((levels, entries, LANES), jnp.float32),
            pltpu.VMEM((entries, LANES), jnp.int32),
            pltpu.SMEM((entries, LANES), jnp.int32),
            pltpu.SemaphoreType.DMA,
        ],
        cost_estimate=pl.CostEstimate(
            flops=8 * levels * blocks * entries * (own + half) * TILE * TILE,
            bytes_accessed=4 * entries * (own + half) * TILE + 16 * blocks * TILE * TILE,
            transcendentals=0,
        ),
        compiler_params=pltpu.CompilerParams(vmem_limit_bytes=32 << 20),
        name="levels",
    )(depth_id, lat_id, *waves, *tails, pool, remote_own, remote_half)
    spread = spread.reshape(levels * lat_size * freq_size, rows, LANES)
    parts = lax.all_to_all(spread, ("depth", "lat", "freq"), 0, 0, tiled=True)
    summed = jnp.sum(parts, axis=0).reshape(1, lateral_width)
    kept = 1.0 - refl
    factor = jnp.where(depth_index == levels - 1, kept * kept, 1.0)
    return summed * factor / (freqs_here * freq_size * shot_total)


def fits_fast(mesh, surface, pool, tile_ids):
    depth, lat, freq = (mesh.shape[name] for name in ("depth", "lat", "freq"))
    freqs, _, shots, width = surface.shape
    rows, slots = tile_ids.shape[1:]
    return (
        depth == 2
        and pool.shape[0] == depth
        and freqs == 3 * freq
        and shots == PACKED * lat
        and TILE == LANES
        and rows * TILE == width
        and rows == SUBLANES * lat
        and 2 * slots < HALF
        and max(rows, pool.shape[2]) <= 256
    )


def solution(mesh):
    placed = (
        P("freq", None, None, "lat"),
        P("depth", "lat"),
        P("depth", "freq", None, None, None),
        P("depth", "lat", None),
        P("depth", "lat", None),
        P("depth", "lat"),
    )

    def whole(surface, refl, pool, tile_ids, block_ids, counts):
        fast = fits_fast(mesh, surface, pool, tile_ids)
        mapped = jax.shard_map(
            per_device_fast if fast else per_device, mesh=mesh, in_specs=placed,
            out_specs=P("depth", "lat"), check_vma=False,
        )
        return mapped(surface, refl, pool, tile_ids, block_ids, counts)

    return whole
```
